32 devices in a mesh: lsec: 4 (over z), rsec: 8 (over y, x, core).
Axes of the slice: x: 2, y: 2, z: 4, core: 2. Of those that a mesh axis runs over, the one named last changes fastest.
Arguments:
- wavefunction: bfloat16 [4096, 4096], P('lsec', 'rsec'), may hold values from -6 to 6
- left_env: bfloat16 [16, 4096, 1024], P(None, 'lsec'), may hold values from -0.1875 to 0.1875
- right_env: bfloat16 [16, 4096, 512], P(None, 'rsec'), may hold values from -0.25 to 0.25
Outputs:
- hpsi: bfloat16 [4096, 4096], P('lsec', 'rsec')
The draws below stay inside these ranges and needn't reach their ends.
All inputs are finite; a program needn't handle non-finite values.
Results may differ from the reference program's by a relative error of at most 0.0053.
Values may be sent and summed in bfloat16 or wider, within the bound.
No kernel may reach another device: no remote copies, remote signals or barrier semaphores. Data moves between devices by JAX's collectives and lax.ppermute only.
A program may use at most 128 MiB of HBM per device.

```python
import jax
import jax.numpy as jnp

BL = 1024
BR = 512
CHANNELS = 16
DL = 4096
DR = 4096
N_LSEC = 4
N_RSEC = 8


def level_of(stream_key, shape, pieces, low, top_value):
    def one(axis_at, shards_of):
        steps = jax.random.uniform(jax.random.fold_in(jax.random.fold_in(stream_key, 6), axis_at), (shards_of,), jnp.float32, low / len(pieces), top_value / len(pieces))
        return jnp.repeat(jnp.exp(steps), shape[axis_at] // shards_of).reshape((-1,) + (1,) * (len(shape) - axis_at - 1))

    gain = one(*pieces[0])
    for cut in pieces[1:]:
        gain = gain * one(*cut)
    return gain


def gaussian(rng, shape, spread, reach, split=(), kind=jnp.bfloat16):
    values = spread * jax.random.normal(rng, shape, jnp.float32)
    if split:
        values = values * level_of(rng, shape, split, -0.22, 0.18)
    return jnp.clip(values, -reach, reach).astype(kind)


def setup_inputs(seed: int = 0) -> dict:
    arg_keys = jax.random.split(jax.random.key(seed), 4)
    return {
        "wavefunction": gaussian(arg_keys[0], (DL, DR), 1.0, 6.0, ((0, 4), (1, 8))),
        "left_env": gaussian(arg_keys[1], (CHANNELS, DL, BL), BL ** -0.5, 0.1875, ((1, 4),)),
        "right_env": gaussian(arg_keys[2], (CHANNELS, DR, BR), BR ** -0.5, 0.25, ((1, 8),)),
    }


channel_shifts = (0, 1, -1, 0)


def shift_blocks(x, axis, offset):
    if offset == 0:
        return x
    count = x.shape[axis]
    if offset == 1:
        kept = jax.lax.slice_in_dim(x, 1, count, axis=axis)
        pad = jnp.zeros_like(jax.lax.slice_in_dim(x, 0, 1, axis=axis))
        return jnp.concatenate([kept, pad], axis=axis)
    kept = jax.lax.slice_in_dim(x, 0, count - 1, axis=axis)
    pad = jnp.zeros_like(jax.lax.slice_in_dim(x, 0, 1, axis=axis))
    return jnp.concatenate([pad, kept], axis=axis)


def reference(wavefunction, left_env, right_env):
    blocks = wavefunction.astype(jnp.float32).reshape(N_LSEC, BL, N_RSEC, BR)
    left_all = left_env.astype(jnp.float32).reshape(CHANNELS, N_LSEC, BL, BL)
    right_all = right_env.astype(jnp.float32).reshape(CHANNELS, N_RSEC, BR, BR)
    total = jnp.zeros((N_LSEC, BL, N_RSEC, BR), jnp.float32)
    upper_sum = jnp.zeros((N_LSEC, BL, N_RSEC, BR), jnp.float32)
    lower_sum = jnp.zeros((N_LSEC, BL, N_RSEC, BR), jnp.float32)
    for channel in range(CHANNELS):
        offset = channel_shifts[channel % 4]
        moved = shift_blocks(shift_blocks(blocks, 0, offset), 2, offset)
        partial_sum = jnp.einsum("iac,ickb->iakb", left_all[channel], moved)
        partial_sum = partial_sum.astype(jnp.bfloat16).astype(jnp.float32)
        right_moved = shift_blocks(right_all[channel], 0, offset)
        term = jnp.einsum("iakc,kcb->iakb", partial_sum, right_moved)
        if offset == 0:
            total = total + term
        elif offset == 1:
            upper_sum = upper_sum + term
        else:
            lower_sum = lower_sum + term
    upper_sum = jax.lax.optimization_barrier(upper_sum.astype(jnp.bfloat16)).astype(jnp.float32)
    lower_sum = jax.lax.optimization_barrier(lower_sum.astype(jnp.bfloat16)).astype(jnp.float32)
    total = total + upper_sum + lower_sum
    total = total.reshape(N_LSEC * BL, N_RSEC * BR)
    return total.astype(jnp.bfloat16)
```

```python
import functools

import jax
import jax.numpy as jnp
from jax import lax
from jax.experimental import pallas as pl
from jax.experimental.pallas import tpu as pltpu
from jax.sharding import PartitionSpec as P

channel_shifts = (0, 1, -1, 0)
period = len(channel_shifts)
vmem_bytes = 57 << 20


def contract(left_block, block, right_block):
    partial = jnp.dot(left_block, block, preferred_element_type=jnp.float32)
    return jnp.dot(
        partial.astype(jnp.bfloat16), right_block, preferred_element_type=jnp.float32
    )


def local_channel(step):
    return period * (step // 2) + (period - 1) * (step % 2)


def cost(steps, rows, columns):
    macs = steps * (rows * rows * columns + rows * columns * columns)
    moved = 2 * steps * (rows * rows + columns * columns)
    return pl.CostEstimate(flops=2 * macs, bytes_accessed=moved, transcendentals=0)


def local_kernel(psi_ref, left_ref, right_ref, total_ref):
    term = contract(left_ref[0], psi_ref[...], right_ref[0])

    @pl.when(pl.program_id(0) == 0)
    def _():
        total_ref[...] = term

    @pl.when(pl.program_id(0) > 0)
    def _():
        total_ref[...] += term


def local_terms(psi, left_env, right_env, steps):
    rows, columns = psi.shape
    return pl.pallas_call(
        local_kernel,
        name="local_terms",
        grid=(steps,),
        in_specs=[
            pl.BlockSpec((rows, columns), lambda w: (0, 0)),
            pl.BlockSpec((1, rows, rows), lambda w: (local_channel(w), 0, 0)),
            pl.BlockSpec((1, columns, columns), lambda w: (local_channel(w), 0, 0)),
        ],
        out_specs=pl.BlockSpec((rows, columns), lambda w: (0, 0)),
        out_shape=jax.ShapeDtypeStruct((rows, columns), jnp.float32),
        compiler_params=pltpu.CompilerParams(vmem_limit_bytes=vmem_bytes),
        cost_estimate=cost(steps, rows, columns),
    )(psi, left_env, right_env)


def early_kernel(charged, psi_ref, left_ref, right_ref, after_ref, term_ref, total_ref):
    del charged, after_ref
    step = pl.program_id(0)
    term = contract(left_ref[0], psi_ref[...], right_ref[0])

    @pl.when(step == 0)
    def _():
        total_ref[...] = term

    @pl.when(step > 0)
    def _():
        total_ref[...] += term

    @pl.when(step == pl.num_programs(0) - 1)
    def _():
        term_ref[...] = total_ref[...].astype(term_ref.dtype)


def early_terms(charged, psi, left_env, right_env, after):
    rows, columns = psi.shape
    steps = left_env.shape[0] // period
    pick = lambda w, charged: (period * w + charged[0], 0, 0)
    return pl.pallas_call(
        early_kernel,
        name="early_terms",
        grid_spec=pltpu.PrefetchScalarGridSpec(
            num_scalar_prefetch=1,
            grid=(steps,),
            in_specs=[
                pl.BlockSpec((rows, columns), lambda w, charged: (0, 0)),
                pl.BlockSpec((1, rows, rows), pick),
                pl.BlockSpec((1, columns, columns), pick),
                pl.BlockSpec(memory_space=pl.ANY),
            ],
            out_specs=pl.BlockSpec((rows, columns), lambda w, charged: (0, 0)),
            scratch_shapes=[pltpu.VMEM((rows, columns), jnp.float32)],
        ),
        out_shape=jax.ShapeDtypeStruct((rows, columns), jnp.bfloat16),
        compiler_params=pltpu.CompilerParams(vmem_limit_bytes=vmem_bytes),
        cost_estimate=cost(steps, rows, columns),
    )(charged, psi, left_env, right_env, after)


def rest_kernel(first, local, charged, psi_ref, moved_ref, left_ref, own_ref, partner_ref,
                start_ref, after_ref, total_ref):
    del charged, after_ref
    step = pl.program_id(0)

    @pl.when(step == 0)
    def _():
        total_ref[...] = start_ref[...]

    @pl.when(step < local)
    def _():
        total_ref[...] += contract(left_ref[0], psi_ref[...], own_ref[0])

    @pl.when(step >= local)
    def _():
        total_ref[...] += contract(left_ref[0], moved_ref[...], partner_ref[0])


def rest_terms(charged, psi, moved, left_env, right_env, partner_env, start, after, first):
    rows, columns = psi.shape
    channels = left_env.shape[0]
    local, late = channels // 2 - first, channels // period

    def own(w, charged):
        return (local_channel(first + jnp.minimum(w, local - 1)), 0, 0)

    def partner(w, charged):
        return (period * jnp.maximum(w - local, 0) + charged[0], 0, 0)

    def left(w, charged):
        channel = jnp.where(w < local, own(w, charged)[0], partner(w, charged)[0])
        return (channel, 0, 0)

    whole = pl.BlockSpec((rows, columns), lambda w, charged: (0, 0))
    return pl.pallas_call(
        functools.partial(rest_kernel, first, local),
        name="rest_terms",
        grid_spec=pltpu.PrefetchScalarGridSpec(
            num_scalar_prefetch=1,
            grid=(local + late,),
            in_specs=[
                whole,
                whole,
                pl.BlockSpec((1, rows, rows), left),
                pl.BlockSpec((1, columns, columns), own),
                pl.BlockSpec((1, columns, columns), partner),
                whole,
                pl.BlockSpec(memory_space=pl.ANY),
            ],
            out_specs=whole,
        ),
        out_shape=jax.ShapeDtypeStruct((rows, columns), jnp.float32),
        compiler_params=pltpu.CompilerParams(vmem_limit_bytes=vmem_bytes),
        cost_estimate=cost(local + late, rows, columns),
    )(charged, psi, moved, left_env, right_env, partner_env, start, after)


def pairs(left_count, right_count):
    index = lambda i, j: i * right_count + j
    straight, crossed, partner, along = [], [], [], []
    for i in range(left_count):
        for j in range(right_count):
            step = 1 if j % 2 == 0 else -1
            partner.append((index(i, j + step), index(i, j)))
            if 0 <= i + step < left_count:
                straight.append((index(i + step, j), index(i, j)))
                crossed.append((index(i + step, j + step), index(i, j)))
            if 0 <= j - step < right_count:
                along.append((index(i, j), index(i, j - step)))
    return straight, crossed, partner, along


def shards(left_count, right_count, psi, left_env, right_env):
    axes = ("lsec", "rsec")
    straight, crossed, partner, along = pairs(left_count, right_count)
    charged = jnp.reshape(1 + lax.axis_index("rsec") % 2, (1,)).astype(jnp.int32)
    first = 5
    moved = lax.ppermute(psi, axes, straight)
    partner_env = lax.ppermute(right_env, axes, partner)
    total = local_terms(psi, left_env, right_env, first)
    moved, psi_after, total = lax.optimization_barrier((moved, psi, total))
    moved_across = lax.ppermute(psi_after, axes, crossed)
    early = early_terms(charged, moved, left_env, right_env, total)
    received = lax.ppermute(early, axes, along)
    total = rest_terms(
        charged, psi, moved_across, left_env, right_env, partner_env, total, early, first
    )
    return (total + received.astype(jnp.float32)).astype(jnp.bfloat16)


def solution(mesh):
    in_specs = (P("lsec", "rsec"), P(None, "lsec", None), P(None, "rsec", None))
    out_specs = P("lsec", "rsec")
    body = functools.partial(shards, mesh.shape["lsec"], mesh.shape["rsec"])
    return jax.shard_map(body, mesh=mesh, in_specs=in_specs, out_specs=out_specs, check_vma=False)
```

```python
import functools

import jax
import jax.numpy as jnp
from jax import lax
from jax.experimental import pallas as pl
from jax.experimental.pallas import tpu as pltpu
from jax.sharding import PartitionSpec as P


channel_shifts = (0, 1, -1, 0)
period = len(channel_shifts)
halves = 2
local_first = 6
vmem_bytes = 20 << 20
in_vmem = pl.BlockSpec(memory_space=pltpu.VMEM)
in_place = pl.BlockSpec(memory_space=pl.ANY)


def contract(left_block, block, right_block):
    partial = jnp.dot(left_block, block, preferred_element_type=jnp.float32)
    return jnp.dot(
        partial.astype(jnp.bfloat16), right_block, preferred_element_type=jnp.float32
    )


def local_channel(step):
    return period * (step // 2) + (period - 1) * (step % 2)


def cost(steps, rows, inner, columns):
    macs = steps * (rows * inner * columns + rows * columns * columns)
    moved = 2 * steps * (rows * inner + columns * columns)
    return pl.CostEstimate(flops=2 * macs, bytes_accessed=moved, transcendentals=0)


def params():
    return pltpu.CompilerParams(vmem_limit_bytes=vmem_bytes)


def half_rows(ref, half):
    rows = ref.shape[0] // halves
    return pl.ds(pl.multiple_of(half * rows, rows), rows)


def local_kernel(psi_ref, left_ref, right_ref, total_ref):
    rows = half_rows(total_ref, pl.program_id(1))
    old = jnp.where(pl.program_id(0) == 0, 0.0, total_ref[rows, :])
    total_ref[rows, :] = old + contract(left_ref[0], psi_ref[...], right_ref[0])


def local_terms(psi, left_env, right_env, steps):
    rows, columns = psi.shape
    return pl.pallas_call(
        local_kernel,
        name="local_terms",
        grid=(steps, halves),
        in_specs=[
            in_vmem,
            pl.BlockSpec((1, rows // halves, rows), lambda w, h: (local_channel(w), h, 0)),
            pl.BlockSpec((1, columns, columns), lambda w, h: (local_channel(w), 0, 0)),
        ],
        out_specs=in_vmem,
        out_shape=jax.ShapeDtypeStruct((rows, columns), jnp.float32),
        compiler_params=params(),
        cost_estimate=cost(steps, rows, rows, columns),
    )(psi, left_env, right_env)


def early_kernel(charged, psi_ref, left_ref, right_ref, after_ref, term_ref, total_ref):
    del charged, after_ref
    old = jnp.where(pl.program_id(0) == 0, 0.0, total_ref[...])
    total = old + contract(left_ref[0], psi_ref[...], right_ref[0])
    total_ref[...] = total
    term_ref[...] = total.astype(term_ref.dtype)


def early_terms(charged, psi, left_env, right_env, half, after):
    rows, columns = psi.shape
    steps = left_env.shape[0] // period
    part = rows // halves
    return pl.pallas_call(
        early_kernel,
        grid_spec=pltpu.PrefetchScalarGridSpec(
            num_scalar_prefetch=1,
            grid=(steps,),
            in_specs=[
                in_vmem,
                pl.BlockSpec((1, part, rows), lambda w, c: (period * w + c[0], half, 0)),
                pl.BlockSpec((1, columns, columns), lambda w, c: (period * w + c[0], 0, 0)),
                in_place,
            ],
            out_specs=in_vmem,
            scratch_shapes=[pltpu.VMEM((part, columns), jnp.float32)],
        ),
        out_shape=jax.ShapeDtypeStruct((part, columns), jnp.bfloat16),
        compiler_params=params(),
        cost_estimate=cost(steps, part, rows, columns),
    )(charged, psi, left_env, right_env, after)


def rest_kernel(local, charged, psi_ref, moved_ref, left_ref, own_ref, partner_ref,
                start_ref, after_ref, total_ref):
    del charged, after_ref, start_ref
    rows = half_rows(total_ref, pl.program_id(1))
    step = pl.program_id(0)

    @pl.when(step < local)
    def _():
        total_ref[rows, :] += contract(left_ref[0], psi_ref[...], own_ref[0])

    @pl.when(step >= local)
    def _():
        total_ref[rows, :] += contract(left_ref[0], moved_ref[...], partner_ref[0])


def rest_terms(charged, psi, moved, left_env, right_env, partner_env, start, after):
    rows, columns = psi.shape
    channels = left_env.shape[0]
    local, late = channels // 2 - local_first, channels // period

    def own(w):
        return local_channel(local_first + jnp.minimum(w, local - 1))

    def partner(w, charged):
        return period * jnp.maximum(w - local, 0) + charged[0]

    def left(w, h, charged):
        return (jnp.where(w < local, own(w), partner(w, charged)), h, 0)

    return pl.pallas_call(
        functools.partial(rest_kernel, local),
        name="rest_terms",
        grid_spec=pltpu.PrefetchScalarGridSpec(
            num_scalar_prefetch=1,
            grid=(local + late, halves),
            in_specs=[
                in_vmem,
                in_vmem,
                pl.BlockSpec((1, rows // halves, rows), left),
                pl.BlockSpec((1, columns, columns), lambda w, h, c: (own(w), 0, 0)),
                pl.BlockSpec((1, columns, columns), lambda w, h, c: (partner(w, c), 0, 0)),
                in_vmem,
                in_place,
            ],
            out_specs=in_vmem,
        ),
        out_shape=jax.ShapeDtypeStruct((rows, columns), jnp.float32),
        input_output_aliases={6: 0},
        compiler_params=params(),
        cost_estimate=cost(local + late, rows, rows, columns),
    )(charged, psi, moved, left_env, right_env, partner_env, start, after)


def finish_kernel(total_ref, first_ref, second_ref, out_ref):
    step = pl.program_id(0)
    rows = out_ref.shape[0]
    steps = pl.num_programs(0) // halves
    total = total_ref[pl.ds(pl.multiple_of(step * rows, rows), rows), :]
    part = pl.ds(pl.multiple_of(lax.rem(step, steps) * rows, rows), rows)

    @pl.when(step < steps)
    def _():
        out_ref[...] = (total + first_ref[part, :].astype(jnp.float32)).astype(out_ref.dtype)

    @pl.when(step >= steps)
    def _():
        out_ref[...] = (total + second_ref[part, :].astype(jnp.float32)).astype(out_ref.dtype)


def finish(total, first, second):
    rows, columns = total.shape
    return pl.pallas_call(
        finish_kernel,
        name="finish",
        grid=(2 * halves,),
        in_specs=[in_vmem, in_vmem, in_vmem],
        out_specs=pl.BlockSpec((rows // (2 * halves), columns), lambda w: (w, 0)),
        out_shape=jax.ShapeDtypeStruct((rows, columns), jnp.bfloat16),
        compiler_params=params(),
    )(total, first, second)


def pairs(left_count, right_count):
    index = lambda i, j: i * right_count + j
    straight, crossed, partner, along = [], [], [], []
    for i in range(left_count):
        for j in range(right_count):
            step = 1 if j % 2 == 0 else -1
            partner.append((index(i, j + step), index(i, j)))
            if 0 <= i + step < left_count:
                straight.append((index(i + step, j), index(i, j)))
                crossed.append((index(i + step, j + step), index(i, j)))
            if 0 <= j - step < right_count:
                along.append((index(i, j), index(i, j - step)))
    return straight, crossed, partner, along


def shards(left_count, right_count, psi, left_env, right_env):
    axes = ("lsec", "rsec")
    straight, crossed, partner, along = pairs(left_count, right_count)
    charged = jnp.reshape(1 + lax.axis_index("rsec") % 2, (1,)).astype(jnp.int32)
    left_env = pltpu.with_memory_space_constraint(left_env, pltpu.HBM)
    right_env = pltpu.with_memory_space_constraint(right_env, pltpu.HBM)
    moved = lax.ppermute(psi, axes, straight)
    partner_env = lax.ppermute(right_env, axes, partner)
    total = local_terms(psi, left_env, right_env, local_first)
    moved, total = lax.optimization_barrier((moved, total))
    first = early_terms(charged, moved, left_env, right_env, 0, total)
    psi_after, first, moved = lax.optimization_barrier((psi, first, moved))
    first_received = lax.ppermute(first, axes, along)
    moved_across = lax.ppermute(psi_after, axes, crossed)
    second = early_terms(charged, moved, left_env, right_env, 1, first)
    second_received = lax.ppermute(second, axes, along)
    total = rest_terms(
        charged, psi, moved_across, left_env, right_env, partner_env, total, second
    )
    return finish(total, first_received, second_received)


def solution(mesh):
    in_specs = (P("lsec", "rsec"), P(None, "lsec", None), P(None, "rsec", None))
    out_specs = P("lsec", "rsec")
    body = functools.partial(shards, mesh.shape["lsec"], mesh.shape["rsec"])
    return jax.shard_map(
        body, mesh=mesh, in_specs=in_specs, out_specs=out_specs, check_vma=False
    )
```

```python
import functools

import jax
import jax.numpy as jnp
from jax import lax
from jax.experimental import pallas as pl
from jax.experimental.pallas import tpu as pltpu
from jax.sharding import PartitionSpec as P


channel_shifts = (0, 1, -1, 0)
period = len(channel_shifts)
local_first = 6
in_vmem = pl.BlockSpec(memory_space=pltpu.VMEM)
in_smem = pl.BlockSpec(memory_space=pltpu.SMEM)
in_hbm = pl.BlockSpec(memory_space=pl.ANY)


def contract(left_block, block, right_block):
    partial = jnp.dot(left_block, block, preferred_element_type=jnp.float32)
    return jnp.dot(
        partial.astype(jnp.bfloat16), right_block, preferred_element_type=jnp.float32
    )


def local_channel(step):
    return period * (step // 2) + (period - 1) * (step % 2)


def cost(steps, rows, inner, columns):
    macs = steps * (rows * inner * columns + rows * columns * columns)
    moved = 2 * steps * (rows * inner + columns * columns)
    return pl.CostEstimate(flops=2 * macs, bytes_accessed=moved, transcendentals=0)


class Fetch:
    def __init__(self, sems):
        self.sems, self.used = sems, 0

    def start(self, *pairs):
        copies = []
        for source, target in pairs:
            copies.append(pltpu.make_async_copy(source, target, self.sems.at[self.used]))
            self.used += 1
        for copy in copies:
            copy.start()
        return copies


def wait(copies):
    for copy in copies:
        copy.wait()


def half_blocks(left_ref, target_ref, charged, half):
    steps, part = target_ref.shape[:2]
    return [
        (left_ref.at[period * w + charged, pl.ds(half * part, part), :], target_ref.at[w])
        for w in range(steps)
    ]


def right_blocks(right_ref, target_ref, charged):
    return [
        (right_ref.at[period * w + charged], target_ref.at[w])
        for w in range(target_ref.shape[0])
    ]


def local_blocks(left_ref, right_ref, left_target, right_target, step, slot):
    channel = local_channel(step)
    return [
        (left_ref.at[channel], left_target.at[slot]),
        (right_ref.at[channel], right_target.at[slot]),
    ]


def local_kernel(charged_ref, psi_ref, left0_ref, right0_ref, left_ref, right_ref,
                 total_ref, next_left_ref, next_right_ref, lefts_ref, rights_ref, sems):
    charged = charged_ref[0]
    fetch = Fetch(sems)
    steps = lefts_ref.shape[0] + 1
    bring = lambda step: fetch.start(
        *local_blocks(left_ref, right_ref, lefts_ref, rights_ref, step, step - 1)
    )
    coming = {step: bring(step) for step in range(1, min(3, steps))}
    last = None
    for step in range(steps):
        if step:
            wait(coming[step])
        if step and step + 2 < steps:
            coming[step + 2] = bring(step + 2)
        if step == max(0, steps - 3):
            last = fetch.start(
                *half_blocks(left_ref, next_left_ref, charged, 0),
                *right_blocks(right_ref, next_right_ref, charged),
            )
        left = lefts_ref[step - 1] if step else left0_ref[...]
        right = rights_ref[step - 1] if step else right0_ref[...]
        term = contract(left, psi_ref[...], right)
        total_ref[...] = total_ref[...] + term if step else term
    wait(last)


def early_term(psi_ref, lefts_ref, rights_ref, term_ref, total_ref):
    steps = lefts_ref.shape[0]
    for step in range(steps):
        term = contract(lefts_ref[step], psi_ref[...], rights_ref[step])
        total = total_ref[...] + term if step else term
        if step + 1 < steps:
            total_ref[...] = total
        else:
            term_ref[...] = total.astype(term_ref.dtype)


def first_kernel(charged_ref, psi_ref, lefts_ref, rights_ref, left_ref, after_ref,
                 term_ref, next_left_ref, total_ref, sems):
    del after_ref
    coming = Fetch(sems).start(*half_blocks(left_ref, next_left_ref, charged_ref[0], 1))
    early_term(psi_ref, lefts_ref, rights_ref, term_ref, total_ref)
    wait(coming)


def second_kernel(psi_ref, lefts_ref, rights_ref, left_ref, right_ref, after_ref,
                  term_ref, next_left_ref, next_right_ref, total_ref, sems):
    del after_ref
    fetch, coming = Fetch(sems), []
    for slot in range(next_left_ref.shape[0]):
        coming += fetch.start(*local_blocks(
            left_ref, right_ref, next_left_ref, next_right_ref, local_first + slot, slot))
    early_term(psi_ref, lefts_ref, rights_ref, term_ref, total_ref)
    wait(coming)


def rest_kernel(charged_ref, psi_ref, lefts_ref, rights_ref, right_ref, start_ref, after_ref,
                total_ref, next_right_ref, sems):
    del after_ref
    coming = Fetch(sems).start(*right_blocks(right_ref, next_right_ref, charged_ref[0]))
    for step in range(lefts_ref.shape[0]):
        total = start_ref if step == 0 else total_ref
        total_ref[...] = total[...] + contract(lefts_ref[step], psi_ref[...], rights_ref[step])
    wait(coming)


def late_kernel(psi_ref, upper_ref, lower_ref, rights_ref, start_ref, received_ref,
                out_ref, total_ref, work_ref, ready_ref, sem):
    part = total_ref.shape[0]
    steps = rights_ref.shape[0]
    put = pltpu.make_async_copy(ready_ref, out_ref.at[pl.ds(0, part), :], sem)
    for half, lefts_ref in enumerate((upper_ref, lower_ref)):
        for step in range(steps):
            old = start_ref[half * part:(half + 1) * part, :] if step == 0 else work_ref[...]
            total = old + contract(lefts_ref[step], psi_ref[...], rights_ref[step])
            if step + 1 < steps:
                work_ref[...] = total
            elif half:
                total_ref[...] = total
            else:
                total = total + received_ref[...].astype(jnp.float32)
                ready_ref[...] = total.astype(ready_ref.dtype)
                put.start()
    put.wait()


def finish_kernel(total_ref, received_ref, start_ref, out_ref, ready_ref, sem):
    del start_ref
    part = total_ref.shape[0]
    total = total_ref[...] + received_ref[...].astype(jnp.float32)
    ready_ref[...] = total.astype(ready_ref.dtype)
    put = pltpu.make_async_copy(ready_ref, out_ref.at[pl.ds(part, part), :], sem)
    put.start()
    put.wait()


def pairs(left_count, right_count):
    index = lambda i, j: i * right_count + j
    straight, crossed, partner, along = [], [], [], []
    for i in range(left_count):
        for j in range(right_count):
            step = 1 if j % 2 == 0 else -1
            partner.append((index(i, j + step), index(i, j)))
            if 0 <= i + step < left_count:
                straight.append((index(i + step, j), index(i, j)))
                crossed.append((index(i + step, j + step), index(i, j)))
            if 0 <= j - step < right_count:
                along.append((index(i, j), index(i, j - step)))
    return straight, crossed, partner, along


def shards(left_count, right_count, psi, left_whole, right_whole):
    axes = ("lsec", "rsec")
    straight, crossed, partner, along = pairs(left_count, right_count)
    rows, columns = psi.shape
    channels = left_whole.shape[0]
    charged_count, local_rest = channels // period, channels // 2 - local_first
    part = rows // 2
    f32, bf16 = jnp.float32, jnp.bfloat16
    lefts = lambda count: pltpu.VMEM((count, rows, rows), bf16)
    halves = pltpu.VMEM((charged_count, part, rows), bf16)
    rights = lambda count: pltpu.VMEM((count, columns, columns), bf16)
    shape = lambda ref: jax.ShapeDtypeStruct(ref.shape, ref.dtype)
    sems = lambda count: pltpu.SemaphoreType.DMA((count,))

    def call(kernel, in_specs, outs, scratch, work, limit=20, aliases=None, out_specs=None):
        return pl.pallas_call(
            kernel,
            in_specs=in_specs,
            out_specs=out_specs or [in_vmem] * len(outs),
            out_shape=[shape(out) for out in outs],
            scratch_shapes=scratch,
            input_output_aliases=aliases or {},
            compiler_params=pltpu.CompilerParams(vmem_limit_bytes=limit << 20),
            cost_estimate=work,
        )

    charged = jnp.reshape(1 + lax.axis_index("rsec") % 2, (1,)).astype(jnp.int32)
    left_env = pltpu.with_memory_space_constraint(left_whole, pltpu.HBM)
    right_env = pltpu.with_memory_space_constraint(right_whole, pltpu.HBM)
    total_shape = pltpu.VMEM((rows, columns), f32)
    half_total = pltpu.VMEM((part, columns), f32)
    half_block = pltpu.VMEM((part, columns), bf16)

    moved = lax.ppermute(psi, axes, straight)
    partner_env = lax.ppermute(right_env, axes, partner)

    total, upper, own = call(
        local_kernel,
        [in_smem, in_vmem, in_vmem, in_vmem, in_hbm, in_hbm],
        [total_shape, halves, rights(charged_count)],
        [lefts(local_first - 1), rights(local_first - 1),
         sems(2 * (local_first - 1) + 2 * charged_count)],
        cost(local_first, rows, rows, columns),
    )(charged, psi, left_whole[0], right_whole[0], left_env, right_env)

    moved, total = lax.optimization_barrier((moved, total))
    first, lower = call(
        first_kernel,
        [in_smem, in_vmem, in_vmem, in_vmem, in_hbm, in_hbm],
        [half_block, halves],
        [half_total, sems(charged_count)],
        cost(charged_count, part, rows, columns),
    )(charged, moved, upper, own, left_env, total)

    psi_after, first, moved = lax.optimization_barrier((psi, first, moved))
    first_received = lax.ppermute(first, axes, along)
    moved_across = lax.ppermute(psi_after, axes, crossed)
    second, rest_left, rest_right = call(
        second_kernel,
        [in_vmem, in_vmem, in_vmem, in_hbm, in_hbm, in_hbm],
        [half_block, lefts(local_rest), rights(local_rest)],
        [half_total, sems(2 * local_rest)],
        cost(charged_count, part, rows, columns),
    )(moved, lower, own, left_env, right_env, first)
    second_received = lax.ppermute(second, axes, along)

    total, across = call(
        rest_kernel,
        [in_smem, in_vmem, in_vmem, in_vmem, in_hbm, in_vmem, in_hbm],
        [total_shape, rights(charged_count)],
        [sems(charged_count)],
        cost(local_rest, rows, rows, columns),
        aliases={5: 0},
    )(charged, psi, rest_left, rest_right, partner_env, total, second)
    moved_across, total = lax.optimization_barrier((moved_across, total))
    out, total = call(
        late_kernel,
        [in_vmem] * 6,
        [pltpu.VMEM((rows, columns), bf16), half_total],
        [half_total, half_block, pltpu.SemaphoreType.DMA],
        cost(charged_count, rows, rows, columns),
        out_specs=[in_hbm, in_vmem],
    )(moved_across, upper, lower, across, total, first_received)
    (out,) = call(
        finish_kernel,
        [in_vmem, in_vmem, in_hbm],
        [pltpu.VMEM((rows, columns), bf16)],
        [half_block, pltpu.SemaphoreType.DMA],
        None,
        aliases={2: 0},
        out_specs=[in_hbm],
    )(total, second_received, out)
    return out


def solution(mesh):
    in_specs = (P("lsec", "rsec"), P(None, "lsec", None), P(None, "rsec", None))
    out_specs = P("lsec", "rsec")
    body = functools.partial(shards, mesh.shape["lsec"], mesh.shape["rsec"])
    return jax.shard_map(
        body, mesh=mesh, in_specs=in_specs, out_specs=out_specs, check_vma=False
    )
```

```python
import functools

import jax
import jax.numpy as jnp
from jax import lax
from jax.experimental import pallas as pl
from jax.experimental.pallas import tpu as pltpu
from jax.sharding import PartitionSpec as P


channel_shifts = (0, 1, -1, 0)
period = len(channel_shifts)
local_first = 5
in_vmem = pl.BlockSpec(memory_space=pltpu.VMEM)
in_smem = pl.BlockSpec(memory_space=pltpu.SMEM)
in_hbm = pl.BlockSpec(memory_space=pl.ANY)


def contract(left_block, block, right_block):
    partial = jnp.dot(left_block, block, preferred_element_type=jnp.float32)
    return jnp.dot(
        partial.astype(jnp.bfloat16), right_block, preferred_element_type=jnp.float32
    )


def local_channel(step):
    return period * (step // 2) + (period - 1) * (step % 2)


def cost(steps, rows, inner, columns):
    macs = steps * (rows * inner * columns + rows * columns * columns)
    moved = 2 * steps * (rows * inner + columns * columns)
    return pl.CostEstimate(flops=2 * macs, bytes_accessed=moved, transcendentals=0)


class Fetch:
    def __init__(self, sems):
        self.sems, self.used = sems, 0

    def start(self, *pairs):
        copies = []
        for source, target in pairs:
            copies.append(pltpu.make_async_copy(source, target, self.sems.at[self.used]))
            self.used += 1
        for copy in copies:
            copy.start()
        return copies


def wait(copies):
    for copy in copies:
        copy.wait()


def half_blocks(left_ref, target_ref, charged, half):
    steps, part = target_ref.shape[:2]
    return [
        (left_ref.at[period * w + charged, pl.ds(half * part, part), :], target_ref.at[w])
        for w in range(steps)
    ]


def right_blocks(right_ref, target_ref, charged):
    return [
        (right_ref.at[period * w + charged], target_ref.at[w])
        for w in range(target_ref.shape[0])
    ]


def local_blocks(left_ref, right_ref, left_target, right_target, step, slot):
    channel = local_channel(step)
    return [
        (left_ref.at[channel], left_target.at[slot]),
        (right_ref.at[channel], right_target.at[slot]),
    ]


def local_kernel(charged_ref, whole_ref, left_ref, right_ref, total_ref, psi_ref, next_left_ref,
                 next_right_ref, give_ref, lefts_ref, rights_ref, sems):
    charged = charged_ref[0]
    fetch = Fetch(sems)
    steps = lefts_ref.shape[0]
    part = total_ref.shape[0] // 2
    halves = (pl.ds(0, part), pl.ds(part, part))
    tops = fetch.start((whole_ref, psi_ref))
    tops += fetch.start((left_ref.at[0, halves[0], :], lefts_ref.at[0, halves[0], :]))
    tops += fetch.start((right_ref.at[0], rights_ref.at[0]))
    bottom = fetch.start((left_ref.at[0, halves[1], :], lefts_ref.at[0, halves[1], :]))
    bring = lambda step: fetch.start(
        *local_blocks(left_ref, right_ref, lefts_ref, rights_ref, step, step)
    )
    coming = {step: bring(step) for step in range(1, min(3, steps))}
    for half, copies in zip(halves, (tops, bottom)):
        wait(copies)
        total_ref[half, :] = contract(lefts_ref[0, half, :], psi_ref[...], rights_ref[0])
    last = []
    for step in range(1, steps):
        wait(coming[step])
        if step + 2 < steps:
            coming[step + 2] = bring(step + 2)
        if step == max(1, steps - 3):
            last += fetch.start(*half_blocks(left_ref, next_left_ref, charged, 0))
        if step == max(1, steps - 2):
            last += fetch.start(*right_blocks(right_ref, next_right_ref, charged))
            last += fetch.start(*right_blocks(right_ref, give_ref, period - 1 - charged))
        total_ref[...] += contract(lefts_ref[step], psi_ref[...], rights_ref[step])
    wait(last)


def early_term(psi_ref, lefts_ref, rights_ref, term_ref, total_ref):
    steps = lefts_ref.shape[0]
    for step in range(steps):
        term = contract(lefts_ref[step], psi_ref[...], rights_ref[step])
        total = total_ref[...] + term if step else term
        if step + 1 < steps:
            total_ref[...] = total
        else:
            term_ref[...] = total.astype(term_ref.dtype)


def first_kernel(charged_ref, psi_ref, lefts_ref, rights_ref, left_ref, after_ref,
                 term_ref, next_left_ref, total_ref, sems):
    del after_ref
    coming = Fetch(sems).start(*half_blocks(left_ref, next_left_ref, charged_ref[0], 1))
    early_term(psi_ref, lefts_ref, rights_ref, term_ref, total_ref)
    wait(coming)


def second_kernel(psi_ref, lefts_ref, rights_ref, left_ref, right_ref, after_ref,
                  term_ref, next_left_ref, next_right_ref, total_ref, sems):
    del after_ref
    coming = Fetch(sems).start(*local_blocks(
        left_ref, right_ref, next_left_ref, next_right_ref, local_first, 0))
    early_term(psi_ref, lefts_ref, rights_ref, term_ref, total_ref)
    wait(coming)


def rest_kernel(psi_ref, left0_ref, right0_ref, left_ref, right_ref, start_ref, after_ref,
                total_ref, lefts_ref, rights_ref, sems):
    del after_ref
    fetch = Fetch(sems)
    count = lefts_ref.shape[0]
    coming = [
        fetch.start(*local_blocks(
            left_ref, right_ref, lefts_ref, rights_ref, local_first + 1 + slot, slot))
        for slot in range(count)
    ]
    total_ref[...] = start_ref[...] + contract(left0_ref[0], psi_ref[...], right0_ref[0])
    for slot in range(count):
        wait(coming[slot])
        total_ref[...] += contract(lefts_ref[slot], psi_ref[...], rights_ref[slot])


def late_kernel(psi_ref, upper_ref, lower_ref, rights_ref, start_ref, received_ref,
                out_ref, total_ref, work_ref, ready_ref, sem):
    part = total_ref.shape[0]
    steps = rights_ref.shape[0]
    put = pltpu.make_async_copy(ready_ref, out_ref.at[pl.ds(0, part), :], sem)
    for half, lefts_ref in enumerate((upper_ref, lower_ref)):
        for step in range(steps):
            old = start_ref[half * part:(half + 1) * part, :] if step == 0 else work_ref[...]
            total = old + contract(lefts_ref[step], psi_ref[...], rights_ref[step])
            if step + 1 < steps:
                work_ref[...] = total
            elif half:
                total_ref[...] = total
            else:
                total = total + received_ref[...].astype(jnp.float32)
                ready_ref[...] = total.astype(ready_ref.dtype)
                put.start()
    put.wait()


def finish_kernel(total_ref, received_ref, start_ref, out_ref, ready_ref, sem):
    del start_ref
    part = total_ref.shape[0]
    total = total_ref[...] + received_ref[...].astype(jnp.float32)
    ready_ref[...] = total.astype(ready_ref.dtype)
    put = pltpu.make_async_copy(ready_ref, out_ref.at[pl.ds(part, part), :], sem)
    put.start()
    put.wait()


def pairs(left_count, right_count):
    index = lambda i, j: i * right_count + j
    straight, crossed, partner, along = [], [], [], []
    for i in range(left_count):
        for j in range(right_count):
            step = 1 if j % 2 == 0 else -1
            partner.append((index(i, j + step), index(i, j)))
            if 0 <= i + step < left_count:
                straight.append((index(i + step, j), index(i, j)))
                crossed.append((index(i + step, j + step), index(i, j)))
            if 0 <= j - step < right_count and 0 <= i + step < left_count:
                along.append((index(i, j), index(i, j - step)))
    return straight, crossed, partner, along


def shards(left_count, right_count, psi, left_whole, right_whole):
    axes = ("lsec", "rsec")
    straight, crossed, partner, along = pairs(left_count, right_count)
    rows, columns = psi.shape
    channels = left_whole.shape[0]
    charged_count, local_rest = channels // period, channels // 2 - local_first
    part = rows // 2
    f32, bf16 = jnp.float32, jnp.bfloat16
    lefts = lambda count: pltpu.VMEM((count, rows, rows), bf16)
    halves = pltpu.VMEM((charged_count, part, rows), bf16)
    rights = lambda count: pltpu.VMEM((count, columns, columns), bf16)
    shape = lambda ref: jax.ShapeDtypeStruct(ref.shape, ref.dtype)
    sems = lambda count: pltpu.SemaphoreType.DMA((count,))

    def call(kernel, in_specs, outs, scratch, work, limit=20, aliases=None, out_specs=None):
        return pl.pallas_call(
            kernel,
            in_specs=in_specs,
            out_specs=out_specs or [in_vmem] * len(outs),
            out_shape=[shape(out) for out in outs],
            scratch_shapes=scratch,
            input_output_aliases=aliases or {},
            compiler_params=pltpu.CompilerParams(vmem_limit_bytes=limit << 20),
            cost_estimate=work,
        )

    charged = jnp.reshape(1 + lax.axis_index("rsec") % 2, (1,)).astype(jnp.int32)
    left_env = pltpu.with_memory_space_constraint(left_whole, pltpu.HBM)
    right_env = pltpu.with_memory_space_constraint(right_whole, pltpu.HBM)
    total_shape = pltpu.VMEM((rows, columns), f32)
    half_total = pltpu.VMEM((part, columns), f32)
    half_block = pltpu.VMEM((part, columns), bf16)

    moved = lax.ppermute(psi, axes, straight)

    total, kept, upper, own, give = call(
        local_kernel,
        [in_smem, in_hbm, in_hbm, in_hbm],
        [total_shape, pltpu.VMEM((rows, columns), bf16), halves, rights(charged_count), rights(charged_count)],
        [lefts(local_first), rights(local_first),
         sems(2 * local_first + 2 + 3 * charged_count)],
        cost(local_first, rows, rows, columns),
    )(charged, psi, left_env, right_env)

    psi_after, total = lax.optimization_barrier((psi, total))
    moved_across = lax.ppermute(psi_after, axes, crossed)
    across = lax.ppermute(give, axes, partner)
    moved, total = lax.optimization_barrier((moved, total))
    first, lower = call(
        first_kernel,
        [in_smem, in_vmem, in_vmem, in_vmem, in_hbm, in_hbm],
        [half_block, halves],
        [half_total, sems(charged_count)],
        cost(charged_count, part, rows, columns),
    )(charged, moved, upper, own, left_env, total)
    first_received = lax.ppermute(first, axes, along)

    second, rest_left, rest_right = call(
        second_kernel,
        [in_vmem, in_vmem, in_vmem, in_hbm, in_hbm, in_hbm],
        [half_block, lefts(1), rights(1)],
        [half_total, sems(2)],
        cost(charged_count, part, rows, columns),
    )(moved, lower, own, left_env, right_env, first)
    second_received = lax.ppermute(second, axes, along)

    (total,) = call(
        rest_kernel,
        [in_vmem, in_vmem, in_vmem, in_hbm, in_hbm, in_vmem, in_hbm],
        [total_shape],
        [lefts(local_rest - 1), rights(local_rest - 1), sems(2 * local_rest - 2)],
        cost(local_rest, rows, rows, columns),
        aliases={5: 0},
    )(kept, rest_left, rest_right, left_env, right_env, total, second)
    moved_across, total = lax.optimization_barrier((moved_across, total))
    out, total = call(
        late_kernel,
        [in_vmem] * 6,
        [pltpu.VMEM((rows, columns), bf16), half_total],
        [half_total, half_block, pltpu.SemaphoreType.DMA],
        cost(charged_count, rows, rows, columns),
        out_specs=[in_hbm, in_vmem],
    )(moved_across, upper, lower, across, total, first_received)
    (out,) = call(
        finish_kernel,
        [in_vmem, in_vmem, in_hbm],
        [pltpu.VMEM((rows, columns), bf16)],
        [half_block, pltpu.SemaphoreType.DMA],
        None,
        aliases={2: 0},
        out_specs=[in_hbm],
    )(total, second_received, out)
    return out


def solution(mesh):
    in_specs = (P("lsec", "rsec"), P(None, "lsec", None), P(None, "rsec", None))
    out_specs = P("lsec", "rsec")
    body = functools.partial(shards, mesh.shape["lsec"], mesh.shape["rsec"])
    return jax.shard_map(
        body, mesh=mesh, in_specs=in_specs, out_specs=out_specs, check_vma=False
    )
```

```python
import functools

import jax
import jax.numpy as jnp
from jax import lax
from jax.experimental import pallas as pl
from jax.experimental.pallas import tpu as pltpu
from jax.sharding import PartitionSpec as P


channel_shifts = (0, 1, -1, 0)
period = len(channel_shifts)
local_first = 5
in_vmem = pl.BlockSpec(memory_space=pltpu.VMEM)
in_smem = pl.BlockSpec(memory_space=pltpu.SMEM)
in_hbm = pl.BlockSpec(memory_space=pl.ANY)


def contract(left_block, block, right_block):
    partial = jnp.dot(left_block, block, preferred_element_type=jnp.float32)
    return jnp.dot(
        partial.astype(jnp.bfloat16), right_block, preferred_element_type=jnp.float32
    )


def local_channel(step):
    return period * (step // 2) + (period - 1) * (step % 2)


def cost(steps, rows, inner, columns):
    macs = steps * (rows * inner * columns + rows * columns * columns)
    moved = 2 * steps * (rows * inner + columns * columns)
    return pl.CostEstimate(flops=2 * macs, bytes_accessed=moved, transcendentals=0)


class Fetch:
    def __init__(self, sems):
        self.sems, self.used = sems, 0

    def start(self, *pairs):
        copies = []
        for source, target in pairs:
            copies.append(pltpu.make_async_copy(source, target, self.sems.at[self.used]))
            self.used += 1
        for copy in copies:
            copy.start()
        return copies


def wait(copies):
    for copy in copies:
        copy.wait()


def half_blocks(left_ref, target_ref, charged, half):
    steps, part = target_ref.shape[:2]
    return [
        (left_ref.at[period * w + charged, pl.ds(half * part, part), :], target_ref.at[w])
        for w in range(steps)
    ]


def right_blocks(right_ref, target_ref, charged):
    return [
        (right_ref.at[period * w + charged], target_ref.at[w])
        for w in range(target_ref.shape[0])
    ]


def local_blocks(left_ref, right_ref, left_target, right_target, step, slot):
    channel = local_channel(step)
    return [
        (left_ref.at[channel], left_target.at[slot]),
        (right_ref.at[channel], right_target.at[slot]),
    ]


def local_kernel(charged_ref, whole_ref, left_ref, right_ref, total_ref, psi_ref, next_left_ref,
                 lower_ref, next_right_ref, give_ref, lefts_ref, rights_ref, sems):
    charged = charged_ref[0]
    fetch = Fetch(sems)
    steps = lefts_ref.shape[0]
    bring = lambda step: fetch.start(
        *local_blocks(left_ref, right_ref, lefts_ref, rights_ref, step, step)
    )
    coming = {0: fetch.start((whole_ref, psi_ref)) + bring(0)}
    last = []
    for step in range(steps):
        wait(coming[step])
        for more in range(1, steps) if step == 0 else ():
            coming[more] = bring(more)
        if step == 1:
            last += fetch.start(*right_blocks(right_ref, next_right_ref, charged))
            last += fetch.start(*half_blocks(left_ref, next_left_ref, charged, 0))
            last += fetch.start(*half_blocks(left_ref, lower_ref, charged, 1))
            last += fetch.start(*right_blocks(right_ref, give_ref, period - 1 - charged))
        term = contract(lefts_ref[step], psi_ref[...], rights_ref[step])
        total_ref[...] = total_ref[...] + term if step else term
    wait(last)


def early_term(psi_ref, lefts_ref, rights_ref, term_ref, total_ref):
    steps = lefts_ref.shape[0]
    for step in range(steps):
        term = contract(lefts_ref[step], psi_ref[...], rights_ref[step])
        total = total_ref[...] + term if step else term
        if step + 1 < steps:
            total_ref[...] = total
        else:
            term_ref[...] = total.astype(term_ref.dtype)


def first_kernel(psi_ref, lefts_ref, rights_ref, after_ref, term_ref, total_ref):
    del after_ref
    early_term(psi_ref, lefts_ref, rights_ref, term_ref, total_ref)


def second_kernel(psi_ref, lefts_ref, rights_ref, left_ref, right_ref, after_ref,
                  term_ref, next_left_ref, next_right_ref, total_ref, sems):
    del after_ref
    coming = Fetch(sems).start(*local_blocks(
        left_ref, right_ref, next_left_ref, next_right_ref, local_first, 0))
    early_term(psi_ref, lefts_ref, rights_ref, term_ref, total_ref)
    wait(coming)


def rest_kernel(psi_ref, left0_ref, right0_ref, left_ref, right_ref, start_ref, after_ref,
                total_ref, lefts_ref, rights_ref, sems):
    del after_ref
    fetch = Fetch(sems)
    count = lefts_ref.shape[0]
    coming = [
        fetch.start(*local_blocks(
            left_ref, right_ref, lefts_ref, rights_ref, local_first + 1 + slot, slot))
        for slot in range(count)
    ]
    total_ref[...] = start_ref[...] + contract(left0_ref[0], psi_ref[...], right0_ref[0])
    for slot in range(count):
        wait(coming[slot])
        total_ref[...] += contract(lefts_ref[slot], psi_ref[...], rights_ref[slot])


def late_kernel(psi_ref, upper_ref, lower_ref, rights_ref, start_ref, received_ref,
                out_ref, total_ref, work_ref, ready_ref, sem):
    part = total_ref.shape[0]
    steps = rights_ref.shape[0]
    put = pltpu.make_async_copy(ready_ref, out_ref.at[pl.ds(0, part), :], sem)
    for half, lefts_ref in enumerate((upper_ref, lower_ref)):
        for step in range(steps):
            old = start_ref[half * part:(half + 1) * part, :] if step == 0 else work_ref[...]
            total = old + contract(lefts_ref[step], psi_ref[...], rights_ref[step])
            if step + 1 < steps:
                work_ref[...] = total
            elif half:
                total_ref[...] = total
            else:
                total = total + received_ref[...].astype(jnp.float32)
                ready_ref[...] = total.astype(ready_ref.dtype)
                put.start()
    put.wait()


def finish_kernel(total_ref, received_ref, start_ref, out_ref, ready_ref, sem):
    del start_ref
    part = total_ref.shape[0]
    total = total_ref[...] + received_ref[...].astype(jnp.float32)
    ready_ref[...] = total.astype(ready_ref.dtype)
    put = pltpu.make_async_copy(ready_ref, out_ref.at[pl.ds(part, part), :], sem)
    put.start()
    put.wait()


def routes(left_count, right_count):
    index = lambda i, j: i * right_count + j
    straight, crossed, partner, along = [], [], [], []
    for i in range(left_count):
        for j in range(right_count):
            step = 1 if j % 2 == 0 else -1
            partner.append((index(i, j + step), index(i, j)))
            if 0 <= i + step < left_count:
                straight.append((index(i + step, j), index(i, j)))
                crossed.append((index(i + step, j + step), index(i, j)))
            if 0 <= j - step < right_count and 0 <= i + step < left_count:
                along.append((index(i, j), index(i, j - step)))
    return straight, crossed, partner, along


def shards(left_count, right_count, psi, left_whole, right_whole):
    axes = ("lsec", "rsec")
    straight, crossed, partner, along = routes(left_count, right_count)
    rows, columns = psi.shape
    channels = left_whole.shape[0]
    charged_count, local_rest = channels // period, channels // 2 - local_first
    part = rows // 2
    f32, bf16 = jnp.float32, jnp.bfloat16
    lefts = lambda count: pltpu.VMEM((count, rows, rows), bf16)
    halves = pltpu.VMEM((charged_count, part, rows), bf16)
    rights = lambda count: pltpu.VMEM((count, columns, columns), bf16)
    shape = lambda ref: jax.ShapeDtypeStruct(ref.shape, ref.dtype)
    sems = lambda count: pltpu.SemaphoreType.DMA((count,))

    def call(kernel, in_specs, outs, scratch, work, limit=20, aliases=None, out_specs=None):
        return pl.pallas_call(
            kernel,
            in_specs=in_specs,
            out_specs=out_specs or [in_vmem] * len(outs),
            out_shape=[shape(out) for out in outs],
            scratch_shapes=scratch,
            input_output_aliases=aliases or {},
            compiler_params=pltpu.CompilerParams(vmem_limit_bytes=limit << 20),
            cost_estimate=work,
        )

    charged = jnp.reshape(1 + lax.axis_index("rsec") % 2, (1,)).astype(jnp.int32)
    left_env = pltpu.with_memory_space_constraint(left_whole, pltpu.HBM)
    right_env = pltpu.with_memory_space_constraint(right_whole, pltpu.HBM)
    total_shape = pltpu.VMEM((rows, columns), f32)
    half_total = pltpu.VMEM((part, columns), f32)
    half_block = pltpu.VMEM((part, columns), bf16)

    moved = lax.ppermute(psi, axes, straight)

    total, kept, upper, lower, own, give = call(
        local_kernel,
        [in_smem, in_hbm, in_hbm, in_hbm],
        [total_shape, pltpu.VMEM((rows, columns), bf16), halves, halves, rights(charged_count), rights(charged_count)],
        [lefts(local_first), rights(local_first),
         sems(2 * local_first + 1 + 4 * charged_count)],
        cost(local_first, rows, rows, columns),
    )(charged, pltpu.with_memory_space_constraint(psi, pltpu.HBM), left_env, right_env)

    moved_across = lax.ppermute(kept, axes, crossed)
    moved, total = lax.optimization_barrier((moved, total))
    (first,) = call(
        first_kernel,
        [in_vmem, in_vmem, in_vmem, in_hbm],
        [half_block],
        [half_total],
        cost(charged_count, part, rows, columns),
    )(moved, upper, own, total)
    first_received = lax.ppermute(first, axes, along)

    second, rest_left, rest_right = call(
        second_kernel,
        [in_vmem, in_vmem, in_vmem, in_hbm, in_hbm, in_hbm],
        [half_block, lefts(1), rights(1)],
        [half_total, sems(2)],
        cost(charged_count, part, rows, columns),
    )(moved, lower, own, left_env, right_env, first)
    second_received = lax.ppermute(second, axes, along)
    across = lax.ppermute(give, axes, partner)

    (total,) = call(
        rest_kernel,
        [in_vmem, in_vmem, in_vmem, in_hbm, in_hbm, in_vmem, in_hbm],
        [total_shape],
        [lefts(local_rest - 1), rights(local_rest - 1), sems(2 * local_rest - 2)],
        cost(local_rest, rows, rows, columns),
        aliases={5: 0},
    )(kept, rest_left, rest_right, left_env, right_env, total, second)
    moved_across, total = lax.optimization_barrier((moved_across, total))
    out, total = call(
        late_kernel,
        [in_vmem] * 6,
        [pltpu.VMEM((rows, columns), bf16), half_total],
        [half_total, half_block, pltpu.SemaphoreType.DMA],
        cost(charged_count, rows, rows, columns),
        out_specs=[in_hbm, in_vmem],
    )(moved_across, upper, lower, across, total, first_received)
    (out,) = call(
        finish_kernel,
        [in_vmem, in_vmem, in_hbm],
        [pltpu.VMEM((rows, columns), bf16)],
        [half_block, pltpu.SemaphoreType.DMA],
        None,
        aliases={2: 0},
        out_specs=[in_hbm],
    )(total, second_received, out)
    return out


def solution(mesh):
    in_specs = (P("lsec", "rsec"), P(None, "lsec", None), P(None, "rsec", None))
    out_specs = P("lsec", "rsec")
    body = functools.partial(shards, mesh.shape["lsec"], mesh.shape["rsec"])
    return jax.shard_map(
        body, mesh=mesh, in_specs=in_specs, out_specs=out_specs, check_vma=False
    )
```

```python
import functools

import jax
import jax.numpy as jnp
from jax import lax
from jax.experimental import pallas as pl
from jax.experimental.pallas import tpu as pltpu
from jax.sharding import PartitionSpec as P


channel_shifts = (0, 1, -1, 0)
period = len(channel_shifts)
local_first = 5
first_eighths = 3
in_vmem = pl.BlockSpec(memory_space=pltpu.VMEM)
in_smem = pl.BlockSpec(memory_space=pltpu.SMEM)
in_hbm = pl.BlockSpec(memory_space=pl.ANY)


def contract(left_block, block, right_block):
    partial = jnp.dot(left_block, block, preferred_element_type=jnp.float32)
    return jnp.dot(
        partial.astype(jnp.bfloat16), right_block, preferred_element_type=jnp.float32
    )


def local_channel(step):
    return period * (step // 2) + (period - 1) * (step % 2)


def cost(steps, rows, inner, columns):
    macs = steps * (rows * inner * columns + rows * columns * columns)
    moved = 2 * steps * (rows * inner + columns * columns)
    return pl.CostEstimate(flops=2 * macs, bytes_accessed=moved, transcendentals=0)


class Fetch:
    def __init__(self, sems):
        self.sems, self.used = sems, 0

    def start(self, *pairs):
        copies = []
        for source, target in pairs:
            copies.append(pltpu.make_async_copy(source, target, self.sems.at[self.used]))
            self.used += 1
        for copy in copies:
            copy.start()
        return copies


def wait(copies):
    for copy in copies:
        copy.wait()


def row_blocks(left_ref, target_ref, charged, first_row):
    steps, count = target_ref.shape[:2]
    rows = pl.ds(first_row, count)
    return [
        (left_ref.at[period * w + charged, rows, :], target_ref.at[w]) for w in range(steps)
    ]


def right_blocks(right_ref, target_ref, charged):
    return [
        (right_ref.at[period * w + charged], target_ref.at[w])
        for w in range(target_ref.shape[0])
    ]


def local_blocks(left_ref, right_ref, left_target, right_target, step, slot):
    channel = local_channel(step)
    return [
        (left_ref.at[channel], left_target.at[slot]),
        (right_ref.at[channel], right_target.at[slot]),
    ]


def local_kernel(charged_ref, whole_ref, left_ref, right_ref, total_ref, psi_ref, next_left_ref,
                 lower_ref, next_right_ref, give_ref, lefts_ref, rights_ref, sems):
    charged = charged_ref[0]
    fetch = Fetch(sems)
    steps = lefts_ref.shape[0]
    bring = lambda step: fetch.start(
        *local_blocks(left_ref, right_ref, lefts_ref, rights_ref, step, step)
    )
    coming = {0: fetch.start((whole_ref, psi_ref)) + bring(0)}
    extra = [
        row_blocks(left_ref, next_left_ref, charged, 0),
        row_blocks(left_ref, lower_ref, charged, next_left_ref.shape[1]),
        right_blocks(right_ref, next_right_ref, charged),
        right_blocks(right_ref, give_ref, period - 1 - charged),
    ]
    last = []
    for step in range(steps):
        if step % 2 or step == 0:
            for near in range(step, min(step + 1 + (step > 0), steps)):
                wait(coming[near])
            begin = step + 1 + (step > 0)
            for far in range(begin, min(begin + 2, steps)):
                coming[far] = bring(far)
        if step > 1 and extra:
            last += fetch.start(*extra.pop(0), *extra.pop(0))
        term = contract(lefts_ref[step], psi_ref[...], rights_ref[step])
        total_ref[...] = total_ref[...] + term if step else term
    for blocks in extra:
        last += fetch.start(*blocks)
    wait(last)


def early_term(psi_ref, lefts_ref, rights_ref, term_ref, total_ref):
    steps = lefts_ref.shape[0]
    for step in range(steps):
        term = contract(lefts_ref[step], psi_ref[...], rights_ref[step])
        total = total_ref[...] + term if step else term
        if step + 1 < steps:
            total_ref[...] = total
        else:
            term_ref[...] = total.astype(term_ref.dtype)


def first_kernel(psi_ref, lefts_ref, rights_ref, after_ref, term_ref, total_ref):
    del after_ref
    early_term(psi_ref, lefts_ref, rights_ref, term_ref, total_ref)


def second_kernel(psi_ref, lefts_ref, rights_ref, left_ref, right_ref, after_ref,
                  term_ref, next_left_ref, next_right_ref, total_ref, sems):
    del after_ref
    coming = Fetch(sems).start(*local_blocks(
        left_ref, right_ref, next_left_ref, next_right_ref, local_first, 0))
    early_term(psi_ref, lefts_ref, rights_ref, term_ref, total_ref)
    wait(coming)


def rest_kernel(psi_ref, left0_ref, right0_ref, left_ref, right_ref, start_ref, after_ref,
                total_ref, lefts_ref, rights_ref, sems):
    del after_ref
    fetch = Fetch(sems)
    count = lefts_ref.shape[0]
    coming = [
        fetch.start(*local_blocks(
            left_ref, right_ref, lefts_ref, rights_ref, local_first + 1 + slot, slot))
        for slot in range(count)
    ]
    total_ref[...] = start_ref[...] + contract(left0_ref[0], psi_ref[...], right0_ref[0])
    wait(sum(coming, []))
    for slot in range(count):
        total_ref[...] += contract(lefts_ref[slot], psi_ref[...], rights_ref[slot])


def late_kernel(psi_ref, upper_ref, lower_ref, rights_ref, start_ref, received_ref,
                out_ref, total_ref, work_ref, ready_ref, sem):
    steps = rights_ref.shape[0]
    count = work_ref.shape[0]
    put = pltpu.make_async_copy(ready_ref, out_ref.at[pl.ds(0, count), :], sem)
    for step in range(steps):
        old = work_ref[...] if step else start_ref[:count, :]
        total = old + contract(upper_ref[step], psi_ref[...], rights_ref[step])
        if step + 1 < steps:
            work_ref[...] = total
        else:
            total = total + received_ref[...].astype(jnp.float32)
            ready_ref[...] = total.astype(ready_ref.dtype)
    put.start()
    for step in range(steps):
        old = total_ref[...] if step else start_ref[count:, :]
        total_ref[...] = old + contract(lower_ref[step], psi_ref[...], rights_ref[step])
    put.wait()


def finish_kernel(total_ref, received_ref, start_ref, out_ref, ready_ref, sems):
    del start_ref
    count = total_ref.shape[0]
    first_row, part = out_ref.shape[0] - count, count // 2
    puts = []
    for half in range(2):
        rows = slice(half * part, (half + 1) * part)
        total = total_ref[rows, :] + received_ref[rows, :].astype(jnp.float32)
        ready_ref[rows, :] = total.astype(ready_ref.dtype)
        puts.append(pltpu.make_async_copy(
            ready_ref.at[pl.ds(half * part, part), :],
            out_ref.at[pl.ds(first_row + half * part, part), :],
            sems.at[half],
        ))
        puts[-1].start()
    wait(puts)


def routes(left_count, right_count):
    index = lambda i, j: i * right_count + j
    straight, crossed, partner, along = [], [], [], []
    for i in range(left_count):
        for j in range(right_count):
            step = 1 if j % 2 == 0 else -1
            partner.append((index(i, j + step), index(i, j)))
            if 0 <= i + step < left_count:
                straight.append((index(i + step, j), index(i, j)))
                crossed.append((index(i + step, j + step), index(i, j)))
            if 0 <= j - step < right_count and 0 <= i + step < left_count:
                along.append((index(i, j), index(i, j - step)))
    return straight, crossed, partner, along


def shards(left_count, right_count, psi, left_whole, right_whole):
    axes = ("lsec", "rsec")
    straight, crossed, partner, along = routes(left_count, right_count)
    rows, columns = psi.shape
    channels = left_whole.shape[0]
    charged_count, local_rest = channels // period, channels // 2 - local_first
    above = rows * first_eighths // 8
    below = rows - above
    f32, bf16 = jnp.float32, jnp.bfloat16
    lefts = lambda count: pltpu.VMEM((count, rows, rows), bf16)
    row_parts = [pltpu.VMEM((charged_count, count, rows), bf16) for count in (above, below)]
    rights = lambda count: pltpu.VMEM((count, columns, columns), bf16)
    shape = lambda ref: jax.ShapeDtypeStruct(ref.shape, ref.dtype)
    sems = lambda count: pltpu.SemaphoreType.DMA((count,))

    def call(kernel, in_specs, outs, scratch, work, limit=20, aliases=None, out_specs=None):
        return pl.pallas_call(
            kernel,
            in_specs=in_specs,
            out_specs=out_specs or [in_vmem] * len(outs),
            out_shape=[shape(out) for out in outs],
            scratch_shapes=scratch,
            input_output_aliases=aliases or {},
            compiler_params=pltpu.CompilerParams(vmem_limit_bytes=limit << 20),
            cost_estimate=work,
        )

    charged = jnp.reshape(1 + lax.axis_index("rsec") % 2, (1,)).astype(jnp.int32)
    left_env = pltpu.with_memory_space_constraint(left_whole, pltpu.HBM)
    right_env = pltpu.with_memory_space_constraint(right_whole, pltpu.HBM)
    total_shape = pltpu.VMEM((rows, columns), f32)
    totals = [pltpu.VMEM((count, columns), f32) for count in (above, below)]
    blocks = [pltpu.VMEM((count, columns), bf16) for count in (above, below)]

    moved = lax.ppermute(psi, axes, straight)

    total, kept, upper, lower, own, give = call(
        local_kernel,
        [in_smem, in_hbm, in_hbm, in_hbm],
        [total_shape, pltpu.VMEM((rows, columns), bf16), *row_parts, rights(charged_count),
         rights(charged_count)],
        [lefts(local_first), rights(local_first),
         sems(2 * local_first + 1 + 4 * charged_count)],
        cost(local_first, rows, rows, columns),
    )(charged, pltpu.with_memory_space_constraint(psi, pltpu.HBM), left_env, right_env)

    moved_across = lax.ppermute(kept, axes, crossed)
    moved, total = lax.optimization_barrier((moved, total))
    (first,) = call(
        first_kernel,
        [in_vmem, in_vmem, in_vmem, in_hbm],
        [blocks[0]],
        [totals[0]],
        cost(charged_count, above, rows, columns),
    )(moved, upper, own, total)
    first_received = lax.ppermute(first, axes, along)

    second, rest_left, rest_right = call(
        second_kernel,
        [in_vmem, in_vmem, in_vmem, in_hbm, in_hbm, in_hbm],
        [blocks[1], lefts(1), rights(1)],
        [totals[1], sems(2)],
        cost(charged_count, below, rows, columns),
    )(moved, lower, own, left_env, right_env, first)
    second_received = lax.ppermute(second, axes, along)
    across = lax.ppermute(give, axes, partner)

    (total,) = call(
        rest_kernel,
        [in_vmem, in_vmem, in_vmem, in_hbm, in_hbm, in_vmem, in_hbm],
        [total_shape],
        [lefts(local_rest - 1), rights(local_rest - 1), sems(2 * local_rest - 2)],
        cost(local_rest, rows, rows, columns),
        aliases={5: 0},
    )(kept, rest_left, rest_right, left_env, right_env, total, second)
    moved_across, total = lax.optimization_barrier((moved_across, total))
    out, total = call(
        late_kernel,
        [in_vmem] * 6,
        [pltpu.VMEM((rows, columns), bf16), totals[1]],
        [totals[0], blocks[0], pltpu.SemaphoreType.DMA],
        cost(charged_count, rows, rows, columns),
        out_specs=[in_hbm, in_vmem],
    )(moved_across, upper, lower, across, total, first_received)
    (out,) = call(
        finish_kernel,
        [in_vmem, in_vmem, in_hbm],
        [pltpu.VMEM((rows, columns), bf16)],
        [blocks[1], sems(2)],
        None,
        aliases={2: 0},
        out_specs=[in_hbm],
    )(total, second_received, out)
    return out


def solution(mesh):
    in_specs = (P("lsec", "rsec"), P(None, "lsec", None), P(None, "rsec", None))
    out_specs = P("lsec", "rsec")
    body = functools.partial(shards, mesh.shape["lsec"], mesh.shape["rsec"])
    return jax.shard_map(
        body, mesh=mesh, in_specs=in_specs, out_specs=out_specs, check_vma=False
    )
```

```python
import functools

import jax
import jax.numpy as jnp
from jax import lax
from jax.experimental import pallas as pl
from jax.experimental.pallas import tpu as pltpu
from jax.sharding import PartitionSpec as P


channel_shifts = (0, 1, -1, 0)
period = len(channel_shifts)
local_first = 5
in_vmem = pl.BlockSpec(memory_space=pltpu.VMEM)
in_smem = pl.BlockSpec(memory_space=pltpu.SMEM)
in_hbm = pl.BlockSpec(memory_space=pl.ANY)


def contract(left_block, block, right_block):
    partial = jnp.dot(left_block, block, preferred_element_type=jnp.float32)
    return jnp.dot(
        partial.astype(jnp.bfloat16), right_block, preferred_element_type=jnp.float32
    )


def local_channel(step):
    return period * (step // 2) + (period - 1) * (step % 2)


def cost(steps, rows, inner, columns):
    macs = steps * (rows * inner * columns + rows * columns * columns)
    moved = 2 * steps * (rows * inner + columns * columns)
    return pl.CostEstimate(flops=2 * macs, bytes_accessed=moved, transcendentals=0)


class Fetch:
    def __init__(self, sems):
        self.sems, self.used = sems, 0

    def start(self, *pairs):
        copies = []
        for source, target in pairs:
            copies.append(pltpu.make_async_copy(source, target, self.sems.at[self.used]))
            self.used += 1
        for copy in copies:
            copy.start()
        return copies


def wait(copies):
    for copy in copies:
        copy.wait()


def half_blocks(left_ref, target_ref, charged, half):
    steps, part = target_ref.shape[:2]
    return [
        (left_ref.at[period * w + charged, pl.ds(half * part, part), :], target_ref.at[w])
        for w in range(steps)
    ]


def right_blocks(right_ref, target_ref, charged):
    return [
        (right_ref.at[period * w + charged], target_ref.at[w])
        for w in range(target_ref.shape[0])
    ]


def local_blocks(left_ref, right_ref, left_target, right_target, step, slot):
    channel = local_channel(step)
    return [
        (left_ref.at[channel], left_target.at[slot]),
        (right_ref.at[channel], right_target.at[slot]),
    ]


def local_kernel(charged_ref, whole_ref, left_ref, right_ref, total_ref, psi_ref, next_left_ref,
                 lower_ref, next_right_ref, give_ref, lefts_ref, rights_ref, sems):
    charged = charged_ref[0]
    fetch = Fetch(sems)
    steps = lefts_ref.shape[0]
    bring = lambda step: fetch.start(
        *local_blocks(left_ref, right_ref, lefts_ref, rights_ref, step, step)
    )
    coming = {0: fetch.start((whole_ref, psi_ref)) + bring(0)}
    last = []
    for step in range(steps):
        wait(coming[step])
        for more in range(1, steps) if step == 0 else ():
            coming[more] = bring(more)
        if step == 1:
            last += fetch.start(*right_blocks(right_ref, next_right_ref, charged))
            last += fetch.start(*half_blocks(left_ref, next_left_ref, charged, 0))
            last += fetch.start(*half_blocks(left_ref, lower_ref, charged, 1))
            last += fetch.start(*right_blocks(right_ref, give_ref, period - 1 - charged))
        term = contract(lefts_ref[step], psi_ref[...], rights_ref[step])
        total_ref[...] = total_ref[...] + term if step else term
    wait(last)


def early_term(psi_ref, lefts_ref, rights_ref, term_ref, total_ref):
    steps = lefts_ref.shape[0]
    for step in range(steps):
        term = contract(lefts_ref[step], psi_ref[...], rights_ref[step])
        total = total_ref[...] + term if step else term
        if step + 1 < steps:
            total_ref[...] = total
        else:
            term_ref[...] = total.astype(term_ref.dtype)


def first_kernel(psi_ref, lefts_ref, rights_ref, after_ref, term_ref, total_ref):
    del after_ref
    early_term(psi_ref, lefts_ref, rights_ref, term_ref, total_ref)


def second_kernel(psi_ref, lefts_ref, rights_ref, left_ref, right_ref, after_ref,
                  term_ref, next_left_ref, next_right_ref, total_ref, sems):
    del after_ref
    coming = Fetch(sems).start(*local_blocks(
        left_ref, right_ref, next_left_ref, next_right_ref, local_first, 0))
    early_term(psi_ref, lefts_ref, rights_ref, term_ref, total_ref)
    wait(coming)


def tail_kernel(psi_ref, moved_ref, left0_ref, right0_ref, upper_ref, lower_ref, across_ref,
                left_ref, right_ref, start_ref, after_ref, total_ref, lefts_ref, rights_ref, sems):
    del after_ref
    fetch = Fetch(sems)
    count = lefts_ref.shape[0]
    coming = [
        fetch.start(*local_blocks(
            left_ref, right_ref, lefts_ref, rights_ref, local_first + 1 + slot, slot))
        for slot in range(count)
    ]
    total_ref[...] = start_ref[...] + contract(left0_ref[0], psi_ref[...], right0_ref[0])
    for slot in range(count):
        wait(coming[slot])
        total_ref[...] += contract(lefts_ref[slot], psi_ref[...], rights_ref[slot])
    part = upper_ref.shape[1]
    for step in range(across_ref.shape[0]):
        for rows, side_ref in ((slice(0, part), upper_ref), (slice(part, None), lower_ref)):
            total_ref[rows, :] += contract(side_ref[step], moved_ref[...], across_ref[step])


def finish_kernel(right_count, total_ref, first_ref, relay_ref, second_ref, out_ref, ready_ref,
                  sems):
    part = first_ref.shape[0]
    sector = lax.axis_index("rsec")
    middle = right_count // 2
    inner = (sector == middle - 1) | (sector == middle)
    relayed = inner | (sector == 0) | (sector == right_count - 1)
    first = jnp.where(relayed, relay_ref[...], first_ref[...])
    puts = []
    for half, received in enumerate((first, second_ref[...])):
        rows = pl.ds(half * part, part)
        total = total_ref[rows, :] + received.astype(jnp.float32)
        ready_ref[rows, :] = total.astype(ready_ref.dtype)
        puts.append(pltpu.make_async_copy(
            ready_ref.at[rows, :], out_ref.at[rows, :], sems.at[half]))
        puts[-1].start()
    wait(puts)


def routes(left_count, right_count):
    index = lambda i, j: i * right_count + j
    straight, crossed, partner, along, onward, relay = [], [], [], [], [], []
    middle, edge = right_count // 2, right_count - 1
    via = {middle - 1: edge, middle: 0}
    for i in range(left_count):
        for j in range(right_count):
            step = 1 if j % 2 == 0 else -1
            partner.append((index(i, j + step), index(i, j)))
            if not 0 <= i + step < left_count:
                continue
            straight.append((index(i + step, j), index(i, j)))
            crossed.append((index(i + step, j + step), index(i, j)))
            if 0 <= j - step < right_count:
                along.append((index(i, j), index(i, j - step)))
                onward.append((index(i, j), index(i, via.get(j, j - step))))
                if j in via:
                    relay.append((index(i, via[j]), index(i, j - step)))
    return straight, crossed, partner, along, onward, relay


def shards(left_count, right_count, psi, left_whole, right_whole):
    axes = ("lsec", "rsec")
    straight, crossed, partner, along, onward, relay = routes(left_count, right_count)
    rows, columns = psi.shape
    channels = left_whole.shape[0]
    charged_count, local_rest = channels // period, channels // 2 - local_first
    part = rows // 2
    f32, bf16 = jnp.float32, jnp.bfloat16
    lefts = lambda count: pltpu.VMEM((count, rows, rows), bf16)
    halves = pltpu.VMEM((charged_count, part, rows), bf16)
    rights = lambda count: pltpu.VMEM((count, columns, columns), bf16)
    shape = lambda ref: jax.ShapeDtypeStruct(ref.shape, ref.dtype)
    sems = lambda count: pltpu.SemaphoreType.DMA((count,))

    def call(kernel, in_specs, outs, scratch, work, limit=20, aliases=None, out_specs=None):
        return pl.pallas_call(
            kernel,
            in_specs=in_specs,
            out_specs=out_specs or [in_vmem] * len(outs),
            out_shape=[shape(out) for out in outs],
            scratch_shapes=scratch,
            input_output_aliases=aliases or {},
            compiler_params=pltpu.CompilerParams(vmem_limit_bytes=limit << 20),
            cost_estimate=work,
        )

    charged = jnp.reshape(1 + lax.axis_index("rsec") % 2, (1,)).astype(jnp.int32)
    left_env = pltpu.with_memory_space_constraint(left_whole, pltpu.HBM)
    right_env = pltpu.with_memory_space_constraint(right_whole, pltpu.HBM)
    total_shape = pltpu.VMEM((rows, columns), f32)
    half_total = pltpu.VMEM((part, columns), f32)
    half_block = pltpu.VMEM((part, columns), bf16)

    moved = lax.ppermute(psi, axes, straight)

    total, kept, upper, lower, own, give = call(
        local_kernel,
        [in_smem, in_hbm, in_hbm, in_hbm],
        [total_shape, pltpu.VMEM((rows, columns), bf16), halves, halves, rights(charged_count), rights(charged_count)],
        [lefts(local_first), rights(local_first),
         sems(2 * local_first + 1 + 4 * charged_count)],
        cost(local_first, rows, rows, columns),
    )(charged, pltpu.with_memory_space_constraint(psi, pltpu.HBM), left_env, right_env)

    moved_across = lax.ppermute(kept, axes, crossed)
    moved, total = lax.optimization_barrier((moved, total))
    (first,) = call(
        first_kernel,
        [in_vmem, in_vmem, in_vmem, in_hbm],
        [half_block],
        [half_total],
        cost(charged_count, part, rows, columns),
    )(moved, upper, own, total)
    first_received = lax.ppermute(first, axes, onward)
    across = lax.ppermute(give, axes, partner)

    second, rest_left, rest_right = call(
        second_kernel,
        [in_vmem, in_vmem, in_vmem, in_hbm, in_hbm, in_hbm],
        [half_block, lefts(1), rights(1)],
        [half_total, sems(2)],
        cost(charged_count, part, rows, columns),
    )(moved, lower, own, left_env, right_env, first)
    second_received = lax.ppermute(second, axes, along)
    relayed = lax.ppermute(first_received, axes, relay)

    (total,) = call(
        tail_kernel,
        [in_vmem] * 7 + [in_hbm, in_hbm, in_vmem, in_hbm],
        [total_shape],
        [lefts(local_rest - 1), rights(local_rest - 1), sems(2 * local_rest - 2)],
        cost(local_rest + charged_count, rows, rows, columns),
        aliases={9: 0},
    )(kept, moved_across, rest_left, rest_right, upper, lower, across, left_env, right_env, total,
      second)
    (out,) = call(
        functools.partial(finish_kernel, right_count),
        [in_vmem] * 4,
        [pltpu.VMEM((rows, columns), bf16)],
        [pltpu.VMEM((rows, columns), bf16), sems(2)],
        None,
        out_specs=[in_hbm],
    )(total, first_received, relayed, second_received)
    return out


def solution(mesh):
    in_specs = (P("lsec", "rsec"), P(None, "lsec", None), P(None, "rsec", None))
    out_specs = P("lsec", "rsec")
    body = functools.partial(shards, mesh.shape["lsec"], mesh.shape["rsec"])
    return jax.shard_map(
        body, mesh=mesh, in_specs=in_specs, out_specs=out_specs, check_vma=False
    )
```

```python
import functools

import jax
import jax.numpy as jnp
from jax import lax
from jax.experimental import pallas as pl
from jax.experimental.pallas import tpu as pltpu
from jax.sharding import PartitionSpec as P


channel_shifts = (0, 1, -1, 0)
period = len(channel_shifts)
local_first = 5
in_vmem = pl.BlockSpec(memory_space=pltpu.VMEM)
in_smem = pl.BlockSpec(memory_space=pltpu.SMEM)
in_hbm = pl.BlockSpec(memory_space=pl.ANY)


def contract(left_block, block, right_block):
    partial = jnp.dot(left_block, block, preferred_element_type=jnp.float32)
    return jnp.dot(
        partial.astype(jnp.bfloat16), right_block, preferred_element_type=jnp.float32
    )


def local_channel(step):
    return period * (step // 2) + (period - 1) * (step % 2)


def cost(steps, rows, inner, columns):
    macs = steps * (rows * inner * columns + rows * columns * columns)
    moved = 2 * steps * (rows * inner + columns * columns)
    return pl.CostEstimate(flops=2 * macs, bytes_accessed=moved, transcendentals=0)


class Fetch:
    def __init__(self, sems):
        self.sems, self.used = sems, 0

    def start(self, *pairs):
        copies = []
        for source, target in pairs:
            copies.append(pltpu.make_async_copy(source, target, self.sems.at[self.used]))
            self.used += 1
        for copy in copies:
            copy.start()
        return copies


def wait(copies):
    for copy in copies:
        copy.wait()


def half_blocks(left_ref, target_ref, charged, half):
    steps, part = target_ref.shape[:2]
    return [
        (left_ref.at[period * w + charged, pl.ds(half * part, part), :], target_ref.at[w])
        for w in range(steps)
    ]


def right_blocks(right_ref, target_ref, charged):
    return [
        (right_ref.at[period * w + charged], target_ref.at[w])
        for w in range(target_ref.shape[0])
    ]


def local_blocks(left_ref, right_ref, left_target, right_target, step, slot):
    channel = local_channel(step)
    return [
        (left_ref.at[channel], left_target.at[slot]),
        (right_ref.at[channel], right_target.at[slot]),
    ]


def local_kernel(charged_ref, whole_ref, left_ref, right_ref, total_ref, psi_ref, next_left_ref,
                 lower_ref, next_right_ref, give_ref, lefts_ref, rights_ref, sems):
    charged = charged_ref[0]
    fetch = Fetch(sems)
    steps = lefts_ref.shape[0]
    bring = lambda step: fetch.start(
        *local_blocks(left_ref, right_ref, lefts_ref, rights_ref, step, step)
    )
    coming = {0: fetch.start((whole_ref, psi_ref)) + bring(0)}
    last = []
    for step in range(steps):
        wait(coming[step])
        for more in range(1, steps) if step == 0 else ():
            coming[more] = bring(more)
        if step == 1:
            last += fetch.start(*right_blocks(right_ref, next_right_ref, charged))
            last += fetch.start(*half_blocks(left_ref, next_left_ref, charged, 0))
            last += fetch.start(*half_blocks(left_ref, lower_ref, charged, 1))
            last += fetch.start(*right_blocks(right_ref, give_ref, period - 1 - charged))
        term = contract(lefts_ref[step], psi_ref[...], rights_ref[step])
        total_ref[...] = total_ref[...] + term if step else term
    wait(last)


def early_term(psi_ref, lefts_ref, rights_ref, term_ref, total_ref):
    steps = lefts_ref.shape[0]
    for step in range(steps):
        term = contract(lefts_ref[step], psi_ref[...], rights_ref[step])
        total = total_ref[...] + term if step else term
        if step + 1 < steps:
            total_ref[...] = total
        else:
            term_ref[...] = total.astype(term_ref.dtype)


def first_kernel(psi_ref, lefts_ref, rights_ref, after_ref, term_ref, total_ref):
    del after_ref
    early_term(psi_ref, lefts_ref, rights_ref, term_ref, total_ref)


def second_kernel(psi_ref, lefts_ref, rights_ref, left_ref, right_ref, after_ref,
                  term_ref, next_left_ref, next_right_ref, total_ref, sems):
    del after_ref
    coming = Fetch(sems).start(*local_blocks(
        left_ref, right_ref, next_left_ref, next_right_ref, local_first, 0))
    early_term(psi_ref, lefts_ref, rights_ref, term_ref, total_ref)
    wait(coming)


def rest_kernel(psi_ref, left0_ref, right0_ref, left_ref, right_ref, start_ref, after_ref,
                total_ref, next_left_ref, next_right_ref, lefts_ref, rights_ref, sems):
    del after_ref
    fetch = Fetch(sems)
    count = lefts_ref.shape[0]
    bring = lambda step, left, right, slot: fetch.start(
        *local_blocks(left_ref, right_ref, left, right, local_first + step, slot)
    )
    coming = [bring(1 + slot, lefts_ref, rights_ref, slot) for slot in range(count)]
    last = bring(1 + count, next_left_ref, next_right_ref, 0)
    total_ref[...] = start_ref[...] + contract(left0_ref[0], psi_ref[...], right0_ref[0])
    for slot in range(count):
        wait(coming[slot])
        total_ref[...] += contract(lefts_ref[slot], psi_ref[...], rights_ref[slot])
    wait(last)


def tail_kernel(psi_ref, moved_ref, left0_ref, right0_ref, upper_ref, lower_ref, across_ref,
                start_ref, after_ref, total_ref):
    del after_ref
    total_ref[...] = start_ref[...] + contract(left0_ref[0], psi_ref[...], right0_ref[0])
    part = upper_ref.shape[1]
    for step in range(across_ref.shape[0]):
        for rows, side_ref in ((slice(0, part), upper_ref), (slice(part, None), lower_ref)):
            total_ref[rows, :] += contract(side_ref[step], moved_ref[...], across_ref[step])


def finish_kernel(right_count, total_ref, first_ref, relay_ref, second_ref, out_ref, ready_ref,
                  sems):
    part = first_ref.shape[0]
    sector = lax.axis_index("rsec")
    middle = right_count // 2
    inner = (sector == middle - 1) | (sector == middle)
    relayed = inner | (sector == 0) | (sector == right_count - 1)
    first = jnp.where(relayed, relay_ref[...], first_ref[...])
    puts = []
    for half, received in enumerate((first, second_ref[...])):
        rows = pl.ds(half * part, part)
        total = total_ref[rows, :] + received.astype(jnp.float32)
        ready_ref[rows, :] = total.astype(ready_ref.dtype)
        puts.append(pltpu.make_async_copy(
            ready_ref.at[rows, :], out_ref.at[rows, :], sems.at[half]))
        puts[-1].start()
    wait(puts)


def routes(left_count, right_count):
    index = lambda i, j: i * right_count + j
    straight, crossed, partner, along, onward, relay = [], [], [], [], [], []
    middle, edge = right_count // 2, right_count - 1
    via = {middle - 1: edge, middle: 0}
    for i in range(left_count):
        for j in range(right_count):
            step = 1 if j % 2 == 0 else -1
            partner.append((index(i, j + step), index(i, j)))
            if not 0 <= i + step < left_count:
                continue
            straight.append((index(i + step, j), index(i, j)))
            crossed.append((index(i + step, j + step), index(i, j)))
            if 0 <= j - step < right_count:
                along.append((index(i, j), index(i, j - step)))
                onward.append((index(i, j), index(i, via.get(j, j - step))))
                if j in via:
                    relay.append((index(i, via[j]), index(i, j - step)))
    return straight, crossed, partner, along, onward, relay


def shards(left_count, right_count, psi, left_whole, right_whole):
    axes = ("lsec", "rsec")
    straight, crossed, partner, along, onward, relay = routes(left_count, right_count)
    rows, columns = psi.shape
    channels = left_whole.shape[0]
    charged_count, local_rest = channels // period, channels // 2 - local_first
    part = rows // 2
    f32, bf16 = jnp.float32, jnp.bfloat16
    lefts = lambda count: pltpu.VMEM((count, rows, rows), bf16)
    halves = pltpu.VMEM((charged_count, part, rows), bf16)
    rights = lambda count: pltpu.VMEM((count, columns, columns), bf16)
    shape = lambda ref: jax.ShapeDtypeStruct(ref.shape, ref.dtype)
    sems = lambda count: pltpu.SemaphoreType.DMA((count,))

    def call(kernel, in_specs, outs, scratch, work, limit=20, aliases=None, out_specs=None):
        return pl.pallas_call(
            kernel,
            in_specs=in_specs,
            out_specs=out_specs or [in_vmem] * len(outs),
            out_shape=[shape(out) for out in outs],
            scratch_shapes=scratch,
            input_output_aliases=aliases or {},
            compiler_params=pltpu.CompilerParams(vmem_limit_bytes=limit << 20),
            cost_estimate=work,
        )

    charged = jnp.reshape(1 + lax.axis_index("rsec") % 2, (1,)).astype(jnp.int32)
    left_env = pltpu.with_memory_space_constraint(left_whole, pltpu.HBM)
    right_env = pltpu.with_memory_space_constraint(right_whole, pltpu.HBM)
    total_shape = pltpu.VMEM((rows, columns), f32)
    half_total = pltpu.VMEM((part, columns), f32)
    half_block = pltpu.VMEM((part, columns), bf16)

    moved = lax.ppermute(psi, axes, straight)

    total, kept, upper, lower, own, give = call(
        local_kernel,
        [in_smem, in_hbm, in_hbm, in_hbm],
        [total_shape, pltpu.VMEM((rows, columns), bf16), halves, halves, rights(charged_count), rights(charged_count)],
        [lefts(local_first), rights(local_first),
         sems(2 * local_first + 1 + 4 * charged_count)],
        cost(local_first, rows, rows, columns),
    )(charged, pltpu.with_memory_space_constraint(psi, pltpu.HBM), left_env, right_env)

    moved_across = lax.ppermute(kept, axes, crossed)
    moved, total = lax.optimization_barrier((moved, total))
    (first,) = call(
        first_kernel,
        [in_vmem, in_vmem, in_vmem, in_hbm],
        [half_block],
        [half_total],
        cost(charged_count, part, rows, columns),
    )(moved, upper, own, total)
    first_received = lax.ppermute(first, axes, onward)
    second, rest_left, rest_right = call(
        second_kernel,
        [in_vmem, in_vmem, in_vmem, in_hbm, in_hbm, in_hbm],
        [half_block, lefts(1), rights(1)],
        [half_total, sems(2)],
        cost(charged_count, part, rows, columns),
    )(moved, lower, own, left_env, right_env, first)
    second_received = lax.ppermute(second, axes, along)
    across = lax.ppermute(give, axes, partner)
    total, rest_left, rest_right = call(
        rest_kernel,
        [in_vmem, in_vmem, in_vmem, in_hbm, in_hbm, in_vmem, in_hbm],
        [total_shape, lefts(1), rights(1)],
        [lefts(local_rest - 2), rights(local_rest - 2), sems(2 * local_rest - 2)],
        cost(local_rest - 1, rows, rows, columns),
        aliases={5: 0},
    )(kept, rest_left, rest_right, left_env, right_env, total, second)
    first_received, total = lax.optimization_barrier((first_received, total))
    relayed = lax.ppermute(first_received, axes, relay)

    (total,) = call(
        tail_kernel,
        [in_vmem] * 8 + [in_hbm],
        [total_shape],
        [],
        cost(1 + charged_count, rows, rows, columns),
        aliases={7: 0},
    )(kept, moved_across, rest_left, rest_right, upper, lower, across, total, second)
    (out,) = call(
        functools.partial(finish_kernel, right_count),
        [in_vmem] * 4,
        [pltpu.VMEM((rows, columns), bf16)],
        [pltpu.VMEM((rows, columns), bf16), sems(2)],
        None,
        out_specs=[in_hbm],
    )(total, first_received, relayed, second_received)
    return out


def solution(mesh):
    in_specs = (P("lsec", "rsec"), P(None, "lsec", None), P(None, "rsec", None))
    out_specs = P("lsec", "rsec")
    body = functools.partial(shards, mesh.shape["lsec"], mesh.shape["rsec"])
    return jax.shard_map(
        body, mesh=mesh, in_specs=in_specs, out_specs=out_specs, check_vma=False
    )
```

```python
import functools

import jax
import jax.numpy as jnp
from jax import lax
from jax.experimental import pallas as pl
from jax.experimental.pallas import tpu as pltpu
from jax.sharding import PartitionSpec as P


channel_shifts = (0, 1, -1, 0)
period = len(channel_shifts)
in_vmem = pl.BlockSpec(memory_space=pltpu.VMEM)
in_smem = pl.BlockSpec(memory_space=pltpu.SMEM)
in_hbm = pl.BlockSpec(memory_space=pl.ANY)


def contract(left_block, block, right_block):
    partial = jnp.dot(left_block, block, preferred_element_type=jnp.float32)
    return jnp.dot(
        partial.astype(jnp.bfloat16), right_block, preferred_element_type=jnp.float32
    )


def local_channel(step):
    return period * (step // 2) + (period - 1) * (step % 2)


def cost(steps, rows, inner, columns):
    macs = steps * (rows * inner * columns + rows * columns * columns)
    moved = 2 * steps * (rows * inner + columns * columns)
    return pl.CostEstimate(flops=2 * macs, bytes_accessed=moved, transcendentals=0)


class Fetch:
    def __init__(self, sems):
        self.sems, self.used = sems, 0

    def start(self, *pairs):
        copies = []
        for source, target in pairs:
            copies.append(pltpu.make_async_copy(source, target, self.sems.at[self.used]))
            self.used += 1
        for copy in copies:
            copy.start()
        return copies


def wait(copies):
    for copy in copies:
        copy.wait()


def half_blocks(left_ref, target_ref, charged, half):
    steps, part = target_ref.shape[:2]
    return [
        (left_ref.at[period * w + charged, pl.ds(half * part, part), :], target_ref.at[w])
        for w in range(steps)
    ]


def right_blocks(right_ref, target_ref, charged):
    return [
        (right_ref.at[period * w + charged], target_ref.at[w])
        for w in range(target_ref.shape[0])
    ]


def local_blocks(left_ref, right_ref, left_target, right_target, step, slot):
    channel = local_channel(step)
    return [
        (left_ref.at[channel], left_target.at[slot]),
        (right_ref.at[channel], right_target.at[slot]),
    ]


def local_kernel(charged_ref, whole_ref, left_ref, right_ref, total_ref, psi_ref, next_left_ref,
                 lower_ref, next_right_ref, give_ref, lefts_ref, rights_ref, sems):
    charged = charged_ref[0]
    fetch = Fetch(sems)
    steps = lefts_ref.shape[0]
    bring = lambda step: fetch.start(
        *local_blocks(left_ref, right_ref, lefts_ref, rights_ref, step, step)
    )
    coming = {0: fetch.start((whole_ref, psi_ref)) + bring(0)}
    last = []
    for step in range(steps):
        wait(coming[step])
        for more in range(1, steps) if step == 0 else ():
            coming[more] = bring(more)
        if step == 1:
            last += fetch.start(*right_blocks(right_ref, next_right_ref, charged))
            last += fetch.start(*half_blocks(left_ref, next_left_ref, charged, 0))
            last += fetch.start(*half_blocks(left_ref, lower_ref, charged, 1))
            last += fetch.start(*right_blocks(right_ref, give_ref, period - 1 - charged))
        term = contract(lefts_ref[step], psi_ref[...], rights_ref[step])
        total_ref[...] = total_ref[...] + term if step else term
    wait(last)


def early_term(psi_ref, lefts_ref, rights_ref, term_ref, total_ref):
    steps = lefts_ref.shape[0]
    for step in range(steps):
        term = contract(lefts_ref[step], psi_ref[...], rights_ref[step])
        total = total_ref[...] + term if step else term
        if step + 1 < steps:
            total_ref[...] = total
        else:
            term_ref[...] = total.astype(term_ref.dtype)


def at_edge(right_count):
    sector = lax.axis_index("rsec")
    return (sector == 0) | (sector == right_count - 1)


def early_or_local(edge, step, kept_ref, psi_ref, lefts_ref, rights_ref, left_ref, right_ref,
                   term_ref, total_ref, work_ref, spare_left_ref, spare_right_ref, sems):
    @pl.when(edge)
    def _():
        wait(Fetch(sems).start(*local_blocks(
            left_ref, right_ref, spare_left_ref, spare_right_ref, step, 0)))
        total_ref[...] += contract(spare_left_ref[0], kept_ref[...], spare_right_ref[0])

    @pl.when(jnp.logical_not(edge))
    def _():
        early_term(psi_ref, lefts_ref, rights_ref, term_ref, work_ref)


def first_kernel(right_count, step, kept_ref, psi_ref, lefts_ref, rights_ref, left_ref,
                 right_ref, start_ref, term_ref, total_ref, work_ref, spare_left_ref,
                 spare_right_ref, sems):
    del start_ref
    early_or_local(at_edge(right_count), step, kept_ref, psi_ref, lefts_ref, rights_ref,
                   left_ref, right_ref, term_ref, total_ref, work_ref, spare_left_ref,
                   spare_right_ref, sems)


def second_kernel(right_count, step, next_step, kept_ref, psi_ref, lefts_ref, rights_ref,
                  left_ref, right_ref, start_ref, after_ref, term_ref, total_ref, next_left_ref,
                  next_right_ref, work_ref, spare_left_ref, spare_right_ref, sems, next_sems):
    del start_ref, after_ref
    coming = Fetch(next_sems).start(*local_blocks(
        left_ref, right_ref, next_left_ref, next_right_ref, next_step, 0))
    early_or_local(at_edge(right_count), step, kept_ref, psi_ref, lefts_ref, rights_ref,
                   left_ref, right_ref, term_ref, total_ref, work_ref, spare_left_ref,
                   spare_right_ref, sems)
    wait(coming)


def rest_kernel(next_step, psi_ref, left0_ref, right0_ref, left_ref, right_ref, start_ref,
                after_ref, total_ref, next_left_ref, next_right_ref, sems):
    del start_ref, after_ref
    coming = Fetch(sems).start(*local_blocks(
        left_ref, right_ref, next_left_ref, next_right_ref, next_step, 0))
    total_ref[...] += contract(left0_ref[0], psi_ref[...], right0_ref[0])
    wait(coming)


def tail_kernel(right_count, step, psi_ref, moved_ref, left0_ref, right0_ref, upper_ref,
                lower_ref, across_ref, left_ref, right_ref, start_ref, after_ref, total_ref,
                spare_left_ref, spare_right_ref, sems):
    del start_ref, after_ref

    @pl.when(jnp.logical_not(at_edge(right_count)))
    def _():
        coming = Fetch(sems).start(*local_blocks(
            left_ref, right_ref, spare_left_ref, spare_right_ref, step, 0))
        total_ref[...] += contract(left0_ref[0], psi_ref[...], right0_ref[0])
        wait(coming)
        total_ref[...] += contract(spare_left_ref[0], psi_ref[...], spare_right_ref[0])

    part = upper_ref.shape[1]
    for index in range(across_ref.shape[0]):
        for rows, side_ref in ((slice(0, part), upper_ref), (slice(part, None), lower_ref)):
            total_ref[rows, :] += contract(side_ref[index], moved_ref[...], across_ref[index])


def finish_kernel(right_count, total_ref, first_ref, relay_ref, second_ref, out_ref, ready_ref,
                  sems):
    part = first_ref.shape[0]
    sector = lax.axis_index("rsec")
    middle = right_count // 2
    inner = (sector == middle - 1) | (sector == middle)
    relayed = inner | (sector == 0) | (sector == right_count - 1)
    first = jnp.where(relayed, relay_ref[...], first_ref[...])
    puts = []
    for half, received in enumerate((first, second_ref[...])):
        rows = pl.ds(half * part, part)
        total = total_ref[rows, :] + received.astype(jnp.float32)
        ready_ref[rows, :] = total.astype(ready_ref.dtype)
        puts.append(pltpu.make_async_copy(
            ready_ref.at[rows, :], out_ref.at[rows, :], sems.at[half]))
        puts[-1].start()
    wait(puts)


def routes(left_count, right_count):
    index = lambda i, j: i * right_count + j
    straight, crossed, partner, along, onward, relay = [], [], [], [], [], []
    middle, edge = right_count // 2, right_count - 1
    via = {middle - 1: edge, middle: 0}
    for i in range(left_count):
        for j in range(right_count):
            step = 1 if j % 2 == 0 else -1
            partner.append((index(i, j + step), index(i, j)))
            if not 0 <= i + step < left_count:
                continue
            straight.append((index(i + step, j), index(i, j)))
            crossed.append((index(i + step, j + step), index(i, j)))
            if 0 <= j - step < right_count:
                along.append((index(i, j), index(i, j - step)))
                onward.append((index(i, j), index(i, via.get(j, j - step))))
                if j in via:
                    relay.append((index(i, via[j]), index(i, j - step)))
    return straight, crossed, partner, along, onward, relay


def shards(left_count, right_count, psi, left_whole, right_whole):
    axes = ("lsec", "rsec")
    straight, crossed, partner, along, onward, relay = routes(left_count, right_count)
    rows, columns = psi.shape
    channels = left_whole.shape[0]
    charged_count = channels // period
    local_first = channels // 2 - 3
    part = rows // 2
    f32, bf16 = jnp.float32, jnp.bfloat16
    lefts = lambda count: pltpu.VMEM((count, rows, rows), bf16)
    halves = pltpu.VMEM((charged_count, part, rows), bf16)
    rights = lambda count: pltpu.VMEM((count, columns, columns), bf16)
    shape = lambda ref: jax.ShapeDtypeStruct(ref.shape, ref.dtype)
    sems = lambda count: pltpu.SemaphoreType.DMA((count,))

    def call(kernel, in_specs, outs, scratch, work, limit=20, aliases=None, out_specs=None):
        return pl.pallas_call(
            kernel,
            in_specs=in_specs,
            out_specs=out_specs or [in_vmem] * len(outs),
            out_shape=[shape(out) for out in outs],
            scratch_shapes=scratch,
            input_output_aliases=aliases or {},
            compiler_params=pltpu.CompilerParams(vmem_limit_bytes=limit << 20),
            cost_estimate=work,
        )

    charged = jnp.reshape(1 + lax.axis_index("rsec") % 2, (1,)).astype(jnp.int32)
    left_env = pltpu.with_memory_space_constraint(left_whole, pltpu.HBM)
    right_env = pltpu.with_memory_space_constraint(right_whole, pltpu.HBM)
    total_shape = pltpu.VMEM((rows, columns), f32)
    half_total = pltpu.VMEM((part, columns), f32)
    half_block = pltpu.VMEM((part, columns), bf16)

    moved = lax.ppermute(psi, axes, straight)

    total, kept, upper, lower, own, give = call(
        local_kernel,
        [in_smem, in_hbm, in_hbm, in_hbm],
        [total_shape, pltpu.VMEM((rows, columns), bf16), halves, halves, rights(charged_count), rights(charged_count)],
        [lefts(local_first), rights(local_first),
         sems(2 * local_first + 1 + 4 * charged_count)],
        cost(local_first, rows, rows, columns),
    )(charged, pltpu.with_memory_space_constraint(psi, pltpu.HBM), left_env, right_env)

    moved_across = lax.ppermute(kept, axes, crossed)
    moved, total = lax.optimization_barrier((moved, total))
    first, total = call(
        functools.partial(first_kernel, right_count, local_first + 2),
        [in_vmem] * 4 + [in_hbm, in_hbm, in_vmem],
        [half_block, total_shape],
        [half_total, lefts(1), rights(1), sems(2)],
        cost(charged_count, part, rows, columns),
        aliases={6: 1},
    )(kept, moved, upper, own, left_env, right_env, total)
    first_received = lax.ppermute(first, axes, onward)
    second, total, rest_left, rest_right = call(
        functools.partial(second_kernel, right_count, local_first + 1, local_first),
        [in_vmem] * 4 + [in_hbm, in_hbm, in_vmem, in_hbm],
        [half_block, total_shape, lefts(1), rights(1)],
        [half_total, lefts(1), rights(1), sems(2), sems(2)],
        cost(charged_count, part, rows, columns),
        aliases={6: 1},
    )(kept, moved, lower, own, left_env, right_env, total, first)
    second_received = lax.ppermute(second, axes, along)
    across = lax.ppermute(give, axes, partner)
    total, rest_left, rest_right = call(
        functools.partial(rest_kernel, local_first + 1),
        [in_vmem, in_vmem, in_vmem, in_hbm, in_hbm, in_vmem, in_hbm],
        [total_shape, lefts(1), rights(1)],
        [sems(2)],
        cost(1, rows, rows, columns),
        aliases={5: 0},
    )(kept, rest_left, rest_right, left_env, right_env, total, second)
    first_received, total = lax.optimization_barrier((first_received, total))
    relayed = lax.ppermute(first_received, axes, relay)

    (total,) = call(
        functools.partial(tail_kernel, right_count, local_first + 2),
        [in_vmem] * 7 + [in_hbm, in_hbm, in_vmem, in_hbm],
        [total_shape],
        [lefts(1), rights(1), sems(2)],
        cost(2 + charged_count, rows, rows, columns),
        aliases={9: 0},
    )(kept, moved_across, rest_left, rest_right, upper, lower, across, left_env, right_env, total,
      second)
    (out,) = call(
        functools.partial(finish_kernel, right_count),
        [in_vmem] * 4,
        [pltpu.VMEM((rows, columns), bf16)],
        [pltpu.VMEM((rows, columns), bf16), sems(2)],
        None,
        out_specs=[in_hbm],
    )(total, first_received, relayed, second_received)
    return out


def solution(mesh):
    in_specs = (P("lsec", "rsec"), P(None, "lsec", None), P(None, "rsec", None))
    out_specs = P("lsec", "rsec")
    body = functools.partial(shards, mesh.shape["lsec"], mesh.shape["rsec"])
    return jax.shard_map(
        body, mesh=mesh, in_specs=in_specs, out_specs=out_specs, check_vma=False
    )
```

```python
import functools

import jax
import jax.numpy as jnp
from jax import lax
from jax.experimental import pallas as pl
from jax.experimental.pallas import tpu as pltpu
from jax.sharding import PartitionSpec as P


channel_shifts = (0, 1, -1, 0)
period = len(channel_shifts)
in_vmem = pl.BlockSpec(memory_space=pltpu.VMEM)
in_smem = pl.BlockSpec(memory_space=pltpu.SMEM)
in_hbm = pl.BlockSpec(memory_space=pl.ANY)


def contract(left_block, block, right_block):
    partial = jnp.dot(left_block, block, preferred_element_type=jnp.float32)
    return jnp.dot(
        partial.astype(jnp.bfloat16), right_block, preferred_element_type=jnp.float32
    )


def local_channel(step):
    return period * (step // 2) + (period - 1) * (step % 2)


def cost(steps, rows, inner, columns):
    macs = steps * (rows * inner * columns + rows * columns * columns)
    moved = 2 * steps * (rows * inner + columns * columns)
    return pl.CostEstimate(flops=2 * macs, bytes_accessed=moved, transcendentals=0)


class Fetch:
    def __init__(self, sems):
        self.sems, self.used = sems, 0

    def start(self, *pairs):
        copies = []
        for source, target in pairs:
            copies.append(pltpu.make_async_copy(source, target, self.sems.at[self.used]))
            self.used += 1
        for copy in copies:
            copy.start()
        return copies


def wait(copies):
    for copy in copies:
        copy.wait()


def half_blocks(left_ref, target_ref, charged, half):
    steps, part = target_ref.shape[:2]
    return [
        (left_ref.at[period * w + charged, pl.ds(half * part, part), :], target_ref.at[w])
        for w in range(steps)
    ]


def right_blocks(right_ref, target_ref, charged):
    return [
        (right_ref.at[period * w + charged], target_ref.at[w])
        for w in range(target_ref.shape[0])
    ]


def local_blocks(left_ref, right_ref, left_target, right_target, step, slot):
    channel = local_channel(step)
    return [
        (left_ref.at[channel], left_target.at[slot]),
        (right_ref.at[channel], right_target.at[slot]),
    ]


def local_kernel(charged_ref, whole_ref, left_ref, right_ref, total_ref, psi_ref, next_left_ref,
                 lower_ref, next_right_ref, give_ref, lefts_ref, rights_ref, sems):
    charged = charged_ref[0]
    fetch = Fetch(sems)
    steps = lefts_ref.shape[0]
    bring = lambda step: fetch.start(
        *local_blocks(left_ref, right_ref, lefts_ref, rights_ref, step, step)
    )
    coming = {0: fetch.start((whole_ref, psi_ref)) + bring(0)}
    last = []
    for step in range(steps):
        wait(coming[step])
        for more in range(1, steps) if step == 0 else ():
            coming[more] = bring(more)
        if step == 1:
            last += fetch.start(*right_blocks(right_ref, next_right_ref, charged))
            last += fetch.start(*half_blocks(left_ref, next_left_ref, charged, 0))
            last += fetch.start(*half_blocks(left_ref, lower_ref, charged, 1))
            last += fetch.start(*right_blocks(right_ref, give_ref, period - 1 - charged))
        term = contract(lefts_ref[step], psi_ref[...], rights_ref[step])
        total_ref[...] = total_ref[...] + term if step else term
    wait(last)


def early_term(psi_ref, lefts_ref, rights_ref, term_ref, total_ref):
    steps = lefts_ref.shape[0]
    for step in range(steps):
        term = contract(lefts_ref[step], psi_ref[...], rights_ref[step])
        total = total_ref[...] + term if step else term
        if step + 1 < steps:
            total_ref[...] = total
        else:
            term_ref[...] = total.astype(term_ref.dtype)


def at_edge(right_count):
    sector = lax.axis_index("rsec")
    return (sector == 0) | (sector == right_count - 1)


def early_or_local(early, local, step, kept_ref, psi_ref, lefts_ref, rights_ref, left_ref,
                   right_ref, term_ref, total_ref, work_ref, spare_left_ref, spare_right_ref,
                   sems):
    copies = [
        pltpu.make_async_copy(source, target, sems.at[index])
        for index, (source, target) in enumerate(local_blocks(
            left_ref, right_ref, spare_left_ref, spare_right_ref, step, 0))
    ]

    @pl.when(local)
    def _():
        for copy in copies:
            copy.start()

    @pl.when(early)
    def _():
        early_term(psi_ref, lefts_ref, rights_ref, term_ref, work_ref)

    @pl.when(local)
    def _():
        wait(copies)
        total_ref[...] += contract(spare_left_ref[0], kept_ref[...], spare_right_ref[0])


def takes_more(right_count):
    return at_edge(right_count) | (lax.rem(lax.axis_index("rsec"), 2) == 1)


def first_kernel(right_count, step, kept_ref, psi_ref, lefts_ref, rights_ref, left_ref,
                 right_ref, start_ref, term_ref, total_ref, work_ref, spare_left_ref,
                 spare_right_ref, sems):
    del start_ref
    early_or_local(jnp.logical_not(at_edge(right_count)), takes_more(right_count), step, kept_ref,
                   psi_ref, lefts_ref, rights_ref, left_ref, right_ref, term_ref, total_ref,
                   work_ref, spare_left_ref, spare_right_ref, sems)


def second_kernel(right_count, step, next_step, kept_ref, psi_ref, lefts_ref, rights_ref,
                  left_ref, right_ref, start_ref, after_ref, term_ref, total_ref, next_left_ref,
                  next_right_ref, work_ref, spare_left_ref, spare_right_ref, sems, next_sems):
    del start_ref, after_ref
    coming = Fetch(next_sems).start(*local_blocks(
        left_ref, right_ref, next_left_ref, next_right_ref, next_step, 0))
    edge = at_edge(right_count)
    early_or_local(jnp.logical_not(edge), edge, step, kept_ref, psi_ref, lefts_ref, rights_ref,
                   left_ref, right_ref, term_ref, total_ref, work_ref, spare_left_ref,
                   spare_right_ref, sems)
    wait(coming)


def rest_kernel(next_step, psi_ref, left0_ref, right0_ref, left_ref, right_ref, start_ref,
                after_ref, total_ref, next_left_ref, next_right_ref, sems):
    del start_ref, after_ref
    coming = Fetch(sems).start(*local_blocks(
        left_ref, right_ref, next_left_ref, next_right_ref, next_step, 0))
    total_ref[...] += contract(left0_ref[0], psi_ref[...], right0_ref[0])
    wait(coming)


def tail_kernel(right_count, step, psi_ref, left0_ref, right0_ref, left_ref, right_ref,
                start_ref, after_ref, total_ref, spare_left_ref, spare_right_ref, sems):
    del start_ref, after_ref
    more = jnp.logical_not(takes_more(right_count))
    copies = [
        pltpu.make_async_copy(source, target, sems.at[index])
        for index, (source, target) in enumerate(local_blocks(
            left_ref, right_ref, spare_left_ref, spare_right_ref, step, 0))
    ]

    @pl.when(more)
    def _():
        for copy in copies:
            copy.start()

    @pl.when(jnp.logical_not(at_edge(right_count)))
    def _():
        total_ref[...] += contract(left0_ref[0], psi_ref[...], right0_ref[0])

    @pl.when(more)
    def _():
        wait(copies)
        total_ref[...] += contract(spare_left_ref[0], psi_ref[...], spare_right_ref[0])


def late_kernel(moved_ref, upper_ref, lower_ref, across_ref, start_ref, total_ref):
    del start_ref
    part = upper_ref.shape[1]
    for index in range(across_ref.shape[0]):
        for rows, side_ref in ((slice(0, part), upper_ref), (slice(part, None), lower_ref)):
            total_ref[rows, :] += contract(side_ref[index], moved_ref[...], across_ref[index])


def finish_kernel(right_count, total_ref, first_ref, relay_ref, second_ref, out_ref, ready_ref,
                  sems):
    part = first_ref.shape[0]
    sector = lax.axis_index("rsec")
    middle = right_count // 2
    inner = (sector == middle - 1) | (sector == middle)
    relayed = inner | (sector == 0) | (sector == right_count - 1)
    first = jnp.where(relayed, relay_ref[...], first_ref[...])
    puts = []
    for half, received in enumerate((first, second_ref[...])):
        rows = pl.ds(half * part, part)
        total = total_ref[rows, :] + received.astype(jnp.float32)
        ready_ref[rows, :] = total.astype(ready_ref.dtype)
        puts.append(pltpu.make_async_copy(
            ready_ref.at[rows, :], out_ref.at[rows, :], sems.at[half]))
        puts[-1].start()
    wait(puts)


def routes(left_count, right_count):
    index = lambda i, j: i * right_count + j
    straight, crossed, partner, along, onward, relay = [], [], [], [], [], []
    middle, edge = right_count // 2, right_count - 1
    via = {middle - 1: edge, middle: 0}
    for i in range(left_count):
        for j in range(right_count):
            step = 1 if j % 2 == 0 else -1
            partner.append((index(i, j + step), index(i, j)))
            if not 0 <= i + step < left_count:
                continue
            straight.append((index(i + step, j), index(i, j)))
            crossed.append((index(i + step, j + step), index(i, j)))
            if 0 <= j - step < right_count:
                along.append((index(i, j), index(i, j - step)))
                onward.append((index(i, j), index(i, via.get(j, j - step))))
                if j in via:
                    relay.append((index(i, via[j]), index(i, j - step)))
    return straight, crossed, partner, along, onward, relay


def shards(left_count, right_count, psi, left_whole, right_whole):
    axes = ("lsec", "rsec")
    straight, crossed, partner, along, onward, relay = routes(left_count, right_count)
    rows, columns = psi.shape
    channels = left_whole.shape[0]
    charged_count = channels // period
    local_first = channels // 2 - 3
    part = rows // 2
    f32, bf16 = jnp.float32, jnp.bfloat16
    lefts = lambda count: pltpu.VMEM((count, rows, rows), bf16)
    halves = pltpu.VMEM((charged_count, part, rows), bf16)
    rights = lambda count: pltpu.VMEM((count, columns, columns), bf16)
    shape = lambda ref: jax.ShapeDtypeStruct(ref.shape, ref.dtype)
    sems = lambda count: pltpu.SemaphoreType.DMA((count,))

    def call(kernel, in_specs, outs, scratch, work, limit=20, aliases=None, out_specs=None):
        return pl.pallas_call(
            kernel,
            in_specs=in_specs,
            out_specs=out_specs or [in_vmem] * len(outs),
            out_shape=[shape(out) for out in outs],
            scratch_shapes=scratch,
            input_output_aliases=aliases or {},
            compiler_params=pltpu.CompilerParams(vmem_limit_bytes=limit << 20),
            cost_estimate=work,
        )

    charged = jnp.reshape(1 + lax.axis_index("rsec") % 2, (1,)).astype(jnp.int32)
    left_env = pltpu.with_memory_space_constraint(left_whole, pltpu.HBM)
    right_env = pltpu.with_memory_space_constraint(right_whole, pltpu.HBM)
    total_shape = pltpu.VMEM((rows, columns), f32)
    half_total = pltpu.VMEM((part, columns), f32)
    half_block = pltpu.VMEM((part, columns), bf16)

    moved = lax.ppermute(psi, axes, straight)

    total, kept, upper, lower, own, give = call(
        local_kernel,
        [in_smem, in_hbm, in_hbm, in_hbm],
        [total_shape, pltpu.VMEM((rows, columns), bf16), halves, halves, rights(charged_count), rights(charged_count)],
        [lefts(local_first), rights(local_first),
         sems(2 * local_first + 1 + 4 * charged_count)],
        cost(local_first, rows, rows, columns),
    )(charged, pltpu.with_memory_space_constraint(psi, pltpu.HBM), left_env, right_env)

    moved_across = lax.ppermute(kept, axes, crossed)
    moved, total = lax.optimization_barrier((moved, total))
    first, total = call(
        functools.partial(first_kernel, right_count, local_first + 2),
        [in_vmem] * 4 + [in_hbm, in_hbm, in_vmem],
        [half_block, total_shape],
        [half_total, lefts(1), rights(1), sems(2)],
        cost(charged_count, part, rows, columns),
        aliases={6: 1},
    )(kept, moved, upper, own, left_env, right_env, total)
    first_received = lax.ppermute(first, axes, onward)
    second, total, rest_left, rest_right = call(
        functools.partial(second_kernel, right_count, local_first + 1, local_first),
        [in_vmem] * 4 + [in_hbm, in_hbm, in_vmem, in_hbm],
        [half_block, total_shape, lefts(1), rights(1)],
        [half_total, lefts(1), rights(1), sems(2), sems(2)],
        cost(charged_count, part, rows, columns),
        aliases={6: 1},
    )(kept, moved, lower, own, left_env, right_env, total, first)
    second_received = lax.ppermute(second, axes, along)
    across = lax.ppermute(give, axes, partner)
    total, rest_left, rest_right = call(
        functools.partial(rest_kernel, local_first + 1),
        [in_vmem, in_vmem, in_vmem, in_hbm, in_hbm, in_vmem, in_hbm],
        [total_shape, lefts(1), rights(1)],
        [sems(2)],
        cost(1, rows, rows, columns),
        aliases={5: 0},
    )(kept, rest_left, rest_right, left_env, right_env, total, second)
    first_received, total = lax.optimization_barrier((first_received, total))
    relayed = lax.ppermute(first_received, axes, relay)

    (total,) = call(
        functools.partial(tail_kernel, right_count, local_first + 2),
        [in_vmem] * 3 + [in_hbm, in_hbm, in_vmem, in_hbm],
        [total_shape],
        [lefts(1), rights(1), sems(2)],
        cost(2, rows, rows, columns),
        aliases={5: 0},
    )(kept, rest_left, rest_right, left_env, right_env, total, second)
    moved_across, across, total = lax.optimization_barrier((moved_across, across, total))
    (total,) = call(
        late_kernel,
        [in_vmem] * 5,
        [total_shape],
        [],
        cost(charged_count, rows, rows, columns),
        aliases={4: 0},
    )(moved_across, upper, lower, across, total)
    (out,) = call(
        functools.partial(finish_kernel, right_count),
        [in_vmem] * 4,
        [pltpu.VMEM((rows, columns), bf16)],
        [pltpu.VMEM((rows, columns), bf16), sems(2)],
        None,
        out_specs=[in_hbm],
    )(total, first_received, relayed, second_received)
    return out


def solution(mesh):
    in_specs = (P("lsec", "rsec"), P(None, "lsec", None), P(None, "rsec", None))
    out_specs = P("lsec", "rsec")
    body = functools.partial(shards, mesh.shape["lsec"], mesh.shape["rsec"])
    return jax.shard_map(
        body, mesh=mesh, in_specs=in_specs, out_specs=out_specs, check_vma=False
    )
```

```python
import functools

import jax
import jax.numpy as jnp
from jax import lax
from jax.experimental import pallas as pl
from jax.experimental.pallas import tpu as pltpu
from jax.sharding import PartitionSpec as P


channel_shifts = (0, 1, -1, 0)
period = len(channel_shifts)
in_vmem = pl.BlockSpec(memory_space=pltpu.VMEM)
in_smem = pl.BlockSpec(memory_space=pltpu.SMEM)
in_hbm = pl.BlockSpec(memory_space=pl.ANY)


def contract(left_block, block, right_block):
    partial = jnp.dot(left_block, block, preferred_element_type=jnp.float32)
    return jnp.dot(
        partial.astype(jnp.bfloat16), right_block, preferred_element_type=jnp.float32
    )


def local_channel(step):
    return period * (step // 2) + (period - 1) * (step % 2)


def cost(steps, rows, inner, columns):
    macs = steps * (rows * inner * columns + rows * columns * columns)
    moved = 2 * steps * (rows * inner + columns * columns)
    return pl.CostEstimate(flops=2 * macs, bytes_accessed=moved, transcendentals=0)


class Fetch:
    def __init__(self, sems):
        self.sems, self.used = sems, 0

    def start(self, *pairs):
        copies = []
        for source, target in pairs:
            copies.append(pltpu.make_async_copy(source, target, self.sems.at[self.used]))
            self.used += 1
        for copy in copies:
            copy.start()
        return copies


def wait(copies):
    for copy in copies:
        copy.wait()


def half_blocks(left_ref, target_ref, charged, half):
    steps, part = target_ref.shape[:2]
    return [
        (left_ref.at[period * w + charged, pl.ds(half * part, part), :], target_ref.at[w])
        for w in range(steps)
    ]


def right_blocks(right_ref, target_ref, charged):
    return [
        (right_ref.at[period * w + charged], target_ref.at[w])
        for w in range(target_ref.shape[0])
    ]


def local_blocks(left_ref, right_ref, left_target, right_target, step, slot):
    channel = local_channel(step)
    return [
        (left_ref.at[channel], left_target.at[slot]),
        (right_ref.at[channel], right_target.at[slot]),
    ]


def spare_copies(left_ref, right_ref, left_target, right_target, step, half, sems):
    channel, part = local_channel(step), left_target.shape[0]
    rows = pl.ds(half * part, part)
    return [
        pltpu.make_async_copy(left_ref.at[channel, rows, :], left_target, sems.at[0]),
        pltpu.make_async_copy(right_ref.at[channel], right_target, sems.at[1]),
    ]


def local_kernel(right_count, spare_step, charged_ref, whole_ref, left_ref, right_ref, total_ref, psi_ref, next_left_ref,
                 lower_ref, next_right_ref, give_ref, lefts_ref, rights_ref, spare_left_ref,
                 spare_right_ref, sems, spare_sems):
    charged = charged_ref[0]
    fetch = Fetch(sems)
    steps = lefts_ref.shape[0]
    bring = lambda step: fetch.start(
        *local_blocks(left_ref, right_ref, lefts_ref, rights_ref, step, step)
    )
    coming = {0: fetch.start((whole_ref, psi_ref)) + bring(0)}
    last = []
    more = jnp.logical_not(takes_more(right_count))
    part = spare_left_ref.shape[0]
    spare = spare_copies(left_ref, right_ref, spare_left_ref, spare_right_ref, spare_step, 0,
                         spare_sems)
    for step in range(steps):
        wait(coming[step])
        for later in range(1, steps) if step == 0 else ():
            coming[later] = bring(later)
        if step == 1:
            last += fetch.start(*right_blocks(right_ref, next_right_ref, charged))
            last += fetch.start(*half_blocks(left_ref, next_left_ref, charged, 0))
            last += fetch.start(*half_blocks(left_ref, lower_ref, charged, 1))
            last += fetch.start(*right_blocks(right_ref, give_ref, period - 1 - charged))
        if step == 2:
            @pl.when(more)
            def _():
                for copy in spare:
                    copy.start()

        term = contract(lefts_ref[step], psi_ref[...], rights_ref[step])
        total_ref[...] = total_ref[...] + term if step else term

    @pl.when(more)
    def _():
        wait(spare)
        total_ref[:part, :] += contract(spare_left_ref[...], psi_ref[...], spare_right_ref[...])

    wait(last)


def early_term(psi_ref, lefts_ref, rights_ref, term_ref, total_ref):
    steps = lefts_ref.shape[0]
    for step in range(steps):
        term = contract(lefts_ref[step], psi_ref[...], rights_ref[step])
        total = total_ref[...] + term if step else term
        if step + 1 < steps:
            total_ref[...] = total
        else:
            term_ref[...] = total.astype(term_ref.dtype)


def at_edge(right_count):
    sector = lax.axis_index("rsec")
    return (sector == 0) | (sector == right_count - 1)


def early_or_local(early, local, step, kept_ref, psi_ref, lefts_ref, rights_ref, left_ref,
                   right_ref, term_ref, total_ref, work_ref, spare_left_ref, spare_right_ref,
                   sems):
    copies = [
        pltpu.make_async_copy(source, target, sems.at[index])
        for index, (source, target) in enumerate(local_blocks(
            left_ref, right_ref, spare_left_ref, spare_right_ref, step, 0))
    ]

    @pl.when(local)
    def _():
        for copy in copies:
            copy.start()

    @pl.when(early)
    def _():
        early_term(psi_ref, lefts_ref, rights_ref, term_ref, work_ref)

    @pl.when(local)
    def _():
        wait(copies)
        total_ref[...] += contract(spare_left_ref[0], kept_ref[...], spare_right_ref[0])


def takes_more(right_count):
    return at_edge(right_count) | (lax.rem(lax.axis_index("rsec"), 2) == 1)


def first_kernel(right_count, step, kept_ref, psi_ref, lefts_ref, rights_ref, left_ref,
                 right_ref, start_ref, term_ref, total_ref, work_ref, spare_left_ref,
                 spare_right_ref, sems):
    del start_ref
    early_or_local(jnp.logical_not(at_edge(right_count)), takes_more(right_count), step, kept_ref,
                   psi_ref, lefts_ref, rights_ref, left_ref, right_ref, term_ref, total_ref,
                   work_ref, spare_left_ref, spare_right_ref, sems)


def second_kernel(right_count, step, next_step, kept_ref, psi_ref, lefts_ref, rights_ref,
                  left_ref, right_ref, start_ref, after_ref, term_ref, total_ref, next_left_ref,
                  next_right_ref, work_ref, spare_left_ref, spare_right_ref, sems, next_sems):
    del start_ref, after_ref
    coming = Fetch(next_sems).start(*local_blocks(
        left_ref, right_ref, next_left_ref, next_right_ref, next_step, 0))
    edge = at_edge(right_count)
    early_or_local(jnp.logical_not(edge), edge, step, kept_ref, psi_ref, lefts_ref, rights_ref,
                   left_ref, right_ref, term_ref, total_ref, work_ref, spare_left_ref,
                   spare_right_ref, sems)
    wait(coming)


def rest_kernel(next_step, psi_ref, left0_ref, right0_ref, left_ref, right_ref, start_ref,
                after_ref, total_ref, next_left_ref, next_right_ref, sems):
    del start_ref, after_ref
    coming = Fetch(sems).start(*local_blocks(
        left_ref, right_ref, next_left_ref, next_right_ref, next_step, 0))
    total_ref[...] += contract(left0_ref[0], psi_ref[...], right0_ref[0])
    wait(coming)


def tail_kernel(right_count, step, psi_ref, left0_ref, right0_ref, left_ref, right_ref,
                start_ref, after_ref, total_ref, spare_left_ref, spare_right_ref, sems):
    del start_ref, after_ref
    more = jnp.logical_not(takes_more(right_count))
    part = spare_left_ref.shape[0]
    spare = spare_copies(left_ref, right_ref, spare_left_ref, spare_right_ref, step, 1, sems)

    @pl.when(more)
    def _():
        for copy in spare:
            copy.start()

    @pl.when(jnp.logical_not(at_edge(right_count)))
    def _():
        total_ref[...] += contract(left0_ref[0], psi_ref[...], right0_ref[0])

    @pl.when(more)
    def _():
        wait(spare)
        total_ref[part:, :] += contract(spare_left_ref[...], psi_ref[...], spare_right_ref[...])


def late_kernel(moved_ref, upper_ref, lower_ref, across_ref, start_ref, total_ref):
    del start_ref
    part = upper_ref.shape[1]
    for index in range(across_ref.shape[0]):
        for rows, side_ref in ((slice(0, part), upper_ref), (slice(part, None), lower_ref)):
            total_ref[rows, :] += contract(side_ref[index], moved_ref[...], across_ref[index])


def finish_kernel(right_count, total_ref, first_ref, relay_ref, second_ref, out_ref, ready_ref,
                  sems):
    part = first_ref.shape[0]
    sector = lax.axis_index("rsec")
    middle = right_count // 2
    inner = (sector == middle - 1) | (sector == middle)
    relayed = inner | (sector == 0) | (sector == right_count - 1)
    puts, step = [], part // 2

    def put(offset, rows, received):
        target = pl.ds(offset + rows.start, step)
        total = total_ref[target, :] + received.astype(jnp.float32)
        ready_ref[target, :] = total.astype(ready_ref.dtype)
        puts.append(pltpu.make_async_copy(
            ready_ref.at[target, :], out_ref.at[target, :], sems.at[len(puts)]))
        puts[-1].start()

    pieces = [slice(0, step), slice(step, part)]
    for rows in pieces:
        put(part, rows, second_ref[rows, :])
    for rows in pieces:
        put(0, rows, jnp.where(relayed, relay_ref[rows, :], first_ref[rows, :]))
    wait(puts)


def routes(left_count, right_count):
    index = lambda i, j: i * right_count + j
    straight, crossed, partner, along, onward, relay = [], [], [], [], [], []
    middle, edge = right_count // 2, right_count - 1
    via = {middle - 1: edge, middle: 0}
    for i in range(left_count):
        for j in range(right_count):
            step = 1 if j % 2 == 0 else -1
            partner.append((index(i, j + step), index(i, j)))
            if not 0 <= i + step < left_count:
                continue
            straight.append((index(i + step, j), index(i, j)))
            crossed.append((index(i + step, j + step), index(i, j)))
            if 0 <= j - step < right_count:
                along.append((index(i, j), index(i, j - step)))
                onward.append((index(i, j), index(i, via.get(j, j - step))))
                if j in via:
                    relay.append((index(i, via[j]), index(i, j - step)))
    return straight, crossed, partner, along, onward, relay


def shards(left_count, right_count, psi, left_whole, right_whole):
    axes = ("lsec", "rsec")
    straight, crossed, partner, along, onward, relay = routes(left_count, right_count)
    rows, columns = psi.shape
    channels = left_whole.shape[0]
    charged_count = channels // period
    local_first = channels // 2 - 3
    part = rows // 2
    f32, bf16 = jnp.float32, jnp.bfloat16
    lefts = lambda count: pltpu.VMEM((count, rows, rows), bf16)
    halves = pltpu.VMEM((charged_count, part, rows), bf16)
    rights = lambda count: pltpu.VMEM((count, columns, columns), bf16)
    shape = lambda ref: jax.ShapeDtypeStruct(ref.shape, ref.dtype)
    sems = lambda count: pltpu.SemaphoreType.DMA((count,))

    def call(kernel, in_specs, outs, scratch, work, limit=20, aliases=None, out_specs=None):
        return pl.pallas_call(
            kernel,
            in_specs=in_specs,
            out_specs=out_specs or [in_vmem] * len(outs),
            out_shape=[shape(out) for out in outs],
            scratch_shapes=scratch,
            input_output_aliases=aliases or {},
            compiler_params=pltpu.CompilerParams(vmem_limit_bytes=limit << 20),
            cost_estimate=work,
        )

    charged = jnp.reshape(1 + lax.axis_index("rsec") % 2, (1,)).astype(jnp.int32)
    left_env = pltpu.with_memory_space_constraint(left_whole, pltpu.HBM)
    right_env = pltpu.with_memory_space_constraint(right_whole, pltpu.HBM)
    total_shape = pltpu.VMEM((rows, columns), f32)
    spare = [pltpu.VMEM((part, rows), bf16), pltpu.VMEM((columns, columns), bf16)]
    half_total = pltpu.VMEM((part, columns), f32)
    half_block = pltpu.VMEM((part, columns), bf16)

    moved = lax.ppermute(psi, axes, straight)

    total, kept, upper, lower, own, give = call(
        functools.partial(local_kernel, right_count, local_first + 2),
        [in_smem, in_hbm, in_hbm, in_hbm],
        [total_shape, pltpu.VMEM((rows, columns), bf16), halves, halves, rights(charged_count), rights(charged_count)],
        [lefts(local_first), rights(local_first), *spare,
         sems(2 * local_first + 1 + 4 * charged_count), sems(2)],
        cost(local_first, rows, rows, columns),
    )(charged, pltpu.with_memory_space_constraint(psi, pltpu.HBM), left_env, right_env)

    moved_across = lax.ppermute(kept, axes, crossed)
    moved, total = lax.optimization_barrier((moved, total))
    first, total = call(
        functools.partial(first_kernel, right_count, local_first + 2),
        [in_vmem] * 4 + [in_hbm, in_hbm, in_vmem],
        [half_block, total_shape],
        [half_total, lefts(1), rights(1), sems(2)],
        cost(charged_count, part, rows, columns),
        aliases={6: 1},
    )(kept, moved, upper, own, left_env, right_env, total)
    first_received = lax.ppermute(first, axes, onward)
    second, total, rest_left, rest_right = call(
        functools.partial(second_kernel, right_count, local_first + 1, local_first),
        [in_vmem] * 4 + [in_hbm, in_hbm, in_vmem, in_hbm],
        [half_block, total_shape, lefts(1), rights(1)],
        [half_total, lefts(1), rights(1), sems(2), sems(2)],
        cost(charged_count, part, rows, columns),
        aliases={6: 1},
    )(kept, moved, lower, own, left_env, right_env, total, first)
    second_received = lax.ppermute(second, axes, along)
    across = lax.ppermute(give, axes, partner)
    total, rest_left, rest_right = call(
        functools.partial(rest_kernel, local_first + 1),
        [in_vmem, in_vmem, in_vmem, in_hbm, in_hbm, in_vmem, in_hbm],
        [total_shape, lefts(1), rights(1)],
        [sems(2)],
        cost(1, rows, rows, columns),
        aliases={5: 0},
    )(kept, rest_left, rest_right, left_env, right_env, total, second)
    first_received, total = lax.optimization_barrier((first_received, total))
    relayed = lax.ppermute(first_received, axes, relay)

    (total,) = call(
        functools.partial(tail_kernel, right_count, local_first + 2),
        [in_vmem] * 3 + [in_hbm, in_hbm, in_vmem, in_hbm],
        [total_shape],
        [*spare, sems(2)],
        cost(2, rows, rows, columns),
        aliases={5: 0},
    )(kept, rest_left, rest_right, left_env, right_env, total, second)
    moved_across, across, total = lax.optimization_barrier((moved_across, across, total))
    (total,) = call(
        late_kernel,
        [in_vmem] * 5,
        [total_shape],
        [],
        cost(charged_count, rows, rows, columns),
        aliases={4: 0},
    )(moved_across, upper, lower, across, total)
    (out,) = call(
        functools.partial(finish_kernel, right_count),
        [in_vmem] * 4,
        [pltpu.VMEM((rows, columns), bf16)],
        [pltpu.VMEM((rows, columns), bf16), sems(4)],
        None,
        out_specs=[in_hbm],
    )(total, first_received, relayed, second_received)
    return out


def solution(mesh):
    in_specs = (P("lsec", "rsec"), P(None, "lsec", None), P(None, "rsec", None))
    out_specs = P("lsec", "rsec")
    body = functools.partial(shards, mesh.shape["lsec"], mesh.shape["rsec"])
    return jax.shard_map(
        body, mesh=mesh, in_specs=in_specs, out_specs=out_specs, check_vma=False
    )
```

```python
import functools

import jax
import jax.numpy as jnp
from jax import lax
from jax.experimental import pallas as pl
from jax.experimental.pallas import tpu as pltpu
from jax.sharding import PartitionSpec as P


channel_shifts = (0, 1, -1, 0)
period = len(channel_shifts)
in_vmem = pl.BlockSpec(memory_space=pltpu.VMEM)
in_smem = pl.BlockSpec(memory_space=pltpu.SMEM)
in_hbm = pl.BlockSpec(memory_space=pl.ANY)


def contract(left_block, block, right_block):
    partial = jnp.dot(left_block, block, preferred_element_type=jnp.float32)
    return jnp.dot(
        partial.astype(jnp.bfloat16), right_block, preferred_element_type=jnp.float32
    )


def local_channel(step):
    return period * (step // 2) + (period - 1) * (step % 2)


def cost(steps, rows, inner, columns):
    macs = steps * (rows * inner * columns + rows * columns * columns)
    moved = 2 * steps * (rows * inner + columns * columns)
    return pl.CostEstimate(flops=2 * macs, bytes_accessed=moved, transcendentals=0)


class Fetch:
    def __init__(self, sems):
        self.sems, self.used = sems, 0

    def start(self, *pairs):
        copies = []
        for source, target in pairs:
            copies.append(pltpu.make_async_copy(source, target, self.sems.at[self.used]))
            self.used += 1
        for copy in copies:
            copy.start()
        return copies


def wait(copies):
    for copy in copies:
        copy.wait()


def half_blocks(left_ref, target_ref, charged, half):
    steps, part = target_ref.shape[:2]
    return [
        (left_ref.at[period * w + charged, pl.ds(half * part, part), :], target_ref.at[w])
        for w in range(steps)
    ]


def right_blocks(right_ref, target_ref, charged):
    return [
        (right_ref.at[period * w + charged], target_ref.at[w])
        for w in range(target_ref.shape[0])
    ]


def local_blocks(left_ref, right_ref, left_target, right_target, step, slot):
    channel = local_channel(step)
    return [
        (left_ref.at[channel], left_target.at[slot]),
        (right_ref.at[channel], right_target.at[slot]),
    ]


def spare_copies(left_ref, right_ref, left_target, right_target, step, half, sems):
    channel, part = local_channel(step), left_target.shape[0]
    rows = pl.ds(half * part, part)
    return [
        pltpu.make_async_copy(left_ref.at[channel, rows, :], left_target, sems.at[0]),
        pltpu.make_async_copy(right_ref.at[channel], right_target, sems.at[1]),
    ]


def local_kernel(right_count, spare_step, charged_ref, whole_ref, left_ref, right_ref, total_ref, psi_ref, next_left_ref,
                 lower_ref, next_right_ref, give_ref, lefts_ref, rights_ref, spare_left_ref,
                 spare_right_ref, sems, spare_sems):
    charged = charged_ref[0]
    fetch = Fetch(sems)
    steps = lefts_ref.shape[0]
    bring = lambda step: fetch.start(
        *local_blocks(left_ref, right_ref, lefts_ref, rights_ref, step, step)
    )
    coming = {0: fetch.start((whole_ref, psi_ref)) + bring(0)}
    last = []
    more = jnp.logical_not(takes_more(right_count))
    part = spare_left_ref.shape[0]
    spare = spare_copies(left_ref, right_ref, spare_left_ref, spare_right_ref, spare_step, 0,
                         spare_sems)
    for step in range(steps):
        wait(coming[step])
        for later in range(1, steps) if step == 0 else ():
            coming[later] = bring(later)
        if step == 1:
            last += fetch.start(*right_blocks(right_ref, next_right_ref, charged))
            last += fetch.start(*half_blocks(left_ref, next_left_ref, charged, 0))
            last += fetch.start(*half_blocks(left_ref, lower_ref, charged, 1))
            last += fetch.start(*right_blocks(right_ref, give_ref, period - 1 - charged))
        if step == 2:
            @pl.when(more)
            def _():
                for copy in spare:
                    copy.start()

        term = contract(lefts_ref[step], psi_ref[...], rights_ref[step])
        total_ref[...] = total_ref[...] + term if step else term

    @pl.when(more)
    def _():
        wait(spare)
        total_ref[:part, :] += contract(spare_left_ref[...], psi_ref[...], spare_right_ref[...])

    wait(last)


def early_term(psi_ref, lefts_ref, rights_ref, term_ref, total_ref):
    steps = lefts_ref.shape[0]
    for step in range(steps):
        term = contract(lefts_ref[step], psi_ref[...], rights_ref[step])
        total = total_ref[...] + term if step else term
        if step + 1 < steps:
            total_ref[...] = total
        else:
            term_ref[...] = total.astype(term_ref.dtype)


def at_edge(right_count):
    sector = lax.axis_index("rsec")
    return (sector == 0) | (sector == right_count - 1)


def early_or_local(early, local, whole, step, kept_ref, psi_ref, lefts_ref, rights_ref, left_ref,
                   right_ref, term_ref, total_ref, work_ref, spare_left_ref, spare_right_ref,
                   sems):
    copies = [
        pltpu.make_async_copy(source, target, sems.at[index])
        for index, (source, target) in enumerate(local_blocks(
            left_ref, right_ref, spare_left_ref, spare_right_ref, step, 0))
    ]

    @pl.when(local)
    def _():
        for copy in copies:
            copy.start()

    @pl.when(early)
    def _():
        early_term(psi_ref, lefts_ref, rights_ref, term_ref, work_ref)

    part = term_ref.shape[0]

    @pl.when(local)
    def _():
        wait(copies)
        total_ref[:part, :] += contract(
            spare_left_ref[0, :part, :], kept_ref[...], spare_right_ref[0])

    @pl.when(whole)
    def _():
        total_ref[part:, :] += contract(
            spare_left_ref[0, part:, :], kept_ref[...], spare_right_ref[0])


def takes_more(right_count):
    return at_edge(right_count) | (lax.rem(lax.axis_index("rsec"), 2) == 1)


def first_kernel(right_count, step, kept_ref, psi_ref, lefts_ref, rights_ref, left_ref,
                 right_ref, start_ref, term_ref, total_ref, work_ref, spare_left_ref,
                 spare_right_ref, sems):
    del start_ref
    edge = at_edge(right_count)
    early_or_local(jnp.logical_not(edge), takes_more(right_count), edge, step, kept_ref, psi_ref,
                   lefts_ref, rights_ref, left_ref, right_ref, term_ref, total_ref, work_ref,
                   spare_left_ref, spare_right_ref, sems)


def second_kernel(right_count, step, next_step, kept_ref, psi_ref, lefts_ref, rights_ref,
                  left_ref, right_ref, start_ref, after_ref, term_ref, total_ref, next_left_ref,
                  next_right_ref, work_ref, spare_left_ref, spare_right_ref, sems, next_sems):
    del start_ref, after_ref
    coming = Fetch(next_sems).start(*local_blocks(
        left_ref, right_ref, next_left_ref, next_right_ref, next_step, 0))
    edge = at_edge(right_count)
    early_or_local(jnp.logical_not(edge), edge, edge, step, kept_ref, psi_ref, lefts_ref, rights_ref,
                   left_ref, right_ref, term_ref, total_ref, work_ref, spare_left_ref,
                   spare_right_ref, sems)
    wait(coming)


def rest_kernel(next_step, psi_ref, left0_ref, right0_ref, left_ref, right_ref, start_ref,
                after_ref, total_ref, next_left_ref, next_right_ref, sems):
    del start_ref, after_ref
    coming = Fetch(sems).start(*local_blocks(
        left_ref, right_ref, next_left_ref, next_right_ref, next_step, 0))
    total_ref[...] += contract(left0_ref[0], psi_ref[...], right0_ref[0])
    wait(coming)


def tail_kernel(right_count, step, psi_ref, left0_ref, right0_ref, left_ref, right_ref,
                start_ref, after_ref, total_ref, spare_left_ref, spare_right_ref, sems):
    del start_ref, after_ref
    part = spare_left_ref.shape[0]
    spare = spare_copies(left_ref, right_ref, spare_left_ref, spare_right_ref, step, 1, sems)

    @pl.when(jnp.logical_not(at_edge(right_count)))
    def _():
        for copy in spare:
            copy.start()
        total_ref[...] += contract(left0_ref[0], psi_ref[...], right0_ref[0])
        wait(spare)
        total_ref[part:, :] += contract(spare_left_ref[...], psi_ref[...], spare_right_ref[...])


def late_kernel(moved_ref, upper_ref, lower_ref, across_ref, start_ref, total_ref):
    del start_ref
    part = upper_ref.shape[1]
    for index in range(across_ref.shape[0]):
        for rows, side_ref in ((slice(0, part), upper_ref), (slice(part, None), lower_ref)):
            total_ref[rows, :] += contract(side_ref[index], moved_ref[...], across_ref[index])


def finish_kernel(right_count, total_ref, first_ref, relay_ref, second_ref, out_ref, ready_ref,
                  sems):
    part = first_ref.shape[0]
    sector = lax.axis_index("rsec")
    middle = right_count // 2
    inner = (sector == middle - 1) | (sector == middle)
    relayed = inner | (sector == 0) | (sector == right_count - 1)
    puts, step = [], part // 2

    def put(offset, rows, received):
        target = pl.ds(offset + rows.start, step)
        total = total_ref[target, :] + received.astype(jnp.float32)
        ready_ref[target, :] = total.astype(ready_ref.dtype)
        puts.append(pltpu.make_async_copy(
            ready_ref.at[target, :], out_ref.at[target, :], sems.at[len(puts)]))
        puts[-1].start()

    pieces = [slice(0, step), slice(step, part)]
    for rows in pieces:
        put(part, rows, second_ref[rows, :])
    for rows in pieces:
        put(0, rows, jnp.where(relayed, relay_ref[rows, :], first_ref[rows, :]))
    wait(puts)


def routes(left_count, right_count):
    index = lambda i, j: i * right_count + j
    straight, crossed, partner, along, onward, relay = [], [], [], [], [], []
    middle, edge = right_count // 2, right_count - 1
    via = {middle - 1: edge, middle: 0}
    for i in range(left_count):
        for j in range(right_count):
            step = 1 if j % 2 == 0 else -1
            partner.append((index(i, j + step), index(i, j)))
            if not 0 <= i + step < left_count:
                continue
            straight.append((index(i + step, j), index(i, j)))
            crossed.append((index(i + step, j + step), index(i, j)))
            if 0 <= j - step < right_count:
                along.append((index(i, j), index(i, j - step)))
                onward.append((index(i, j), index(i, via.get(j, j - step))))
                if j in via:
                    relay.append((index(i, via[j]), index(i, j - step)))
    return straight, crossed, partner, along, onward, relay


def shards(left_count, right_count, psi, left_whole, right_whole):
    axes = ("lsec", "rsec")
    straight, crossed, partner, along, onward, relay = routes(left_count, right_count)
    rows, columns = psi.shape
    channels = left_whole.shape[0]
    charged_count = channels // period
    local_first = channels // 2 - 3
    part = rows // 2
    f32, bf16 = jnp.float32, jnp.bfloat16
    lefts = lambda count: pltpu.VMEM((count, rows, rows), bf16)
    halves = pltpu.VMEM((charged_count, part, rows), bf16)
    rights = lambda count: pltpu.VMEM((count, columns, columns), bf16)
    shape = lambda ref: jax.ShapeDtypeStruct(ref.shape, ref.dtype)
    sems = lambda count: pltpu.SemaphoreType.DMA((count,))

    def call(kernel, in_specs, outs, scratch, work, limit=20, aliases=None, out_specs=None):
        return pl.pallas_call(
            kernel,
            in_specs=in_specs,
            out_specs=out_specs or [in_vmem] * len(outs),
            out_shape=[shape(out) for out in outs],
            scratch_shapes=scratch,
            input_output_aliases=aliases or {},
            compiler_params=pltpu.CompilerParams(vmem_limit_bytes=limit << 20),
            cost_estimate=work,
        )

    charged = jnp.reshape(1 + lax.axis_index("rsec") % 2, (1,)).astype(jnp.int32)
    left_env = pltpu.with_memory_space_constraint(left_whole, pltpu.HBM)
    right_env = pltpu.with_memory_space_constraint(right_whole, pltpu.HBM)
    total_shape = pltpu.VMEM((rows, columns), f32)
    spare = [pltpu.VMEM((part, rows), bf16), pltpu.VMEM((columns, columns), bf16)]
    half_total = pltpu.VMEM((part, columns), f32)
    half_block = pltpu.VMEM((part, columns), bf16)

    moved = lax.ppermute(psi, axes, straight)

    total, kept, upper, lower, own, give = call(
        functools.partial(local_kernel, right_count, local_first + 2),
        [in_smem, in_hbm, in_hbm, in_hbm],
        [total_shape, pltpu.VMEM((rows, columns), bf16), halves, halves, rights(charged_count), rights(charged_count)],
        [lefts(local_first), rights(local_first), *spare,
         sems(2 * local_first + 1 + 4 * charged_count), sems(2)],
        cost(local_first, rows, rows, columns),
    )(charged, pltpu.with_memory_space_constraint(psi, pltpu.HBM), left_env, right_env)

    moved_across = lax.ppermute(kept, axes, crossed)
    moved, total = lax.optimization_barrier((moved, total))
    first, total = call(
        functools.partial(first_kernel, right_count, local_first + 2),
        [in_vmem] * 4 + [in_hbm, in_hbm, in_vmem],
        [half_block, total_shape],
        [half_total, lefts(1), rights(1), sems(2)],
        cost(charged_count, part, rows, columns),
        aliases={6: 1},
    )(kept, moved, upper, own, left_env, right_env, total)
    first_received = lax.ppermute(first, axes, onward)
    second, total, rest_left, rest_right = call(
        functools.partial(second_kernel, right_count, local_first + 1, local_first),
        [in_vmem] * 4 + [in_hbm, in_hbm, in_vmem, in_hbm],
        [half_block, total_shape, lefts(1), rights(1)],
        [half_total, lefts(1), rights(1), sems(2), sems(2)],
        cost(charged_count, part, rows, columns),
        aliases={6: 1},
    )(kept, moved, lower, own, left_env, right_env, total, first)
    second_received = lax.ppermute(second, axes, along)
    across = lax.ppermute(give, axes, partner)
    relayed = lax.ppermute(first_received, axes, relay)
    total, rest_left, rest_right = call(
        functools.partial(rest_kernel, local_first + 1),
        [in_vmem, in_vmem, in_vmem, in_hbm, in_hbm, in_vmem, in_hbm],
        [total_shape, lefts(1), rights(1)],
        [sems(2)],
        cost(1, rows, rows, columns),
        aliases={5: 0},
    )(kept, rest_left, rest_right, left_env, right_env, total, second)

    (total,) = call(
        functools.partial(tail_kernel, right_count, local_first + 2),
        [in_vmem] * 3 + [in_hbm, in_hbm, in_vmem, in_hbm],
        [total_shape],
        [*spare, sems(2)],
        cost(2, rows, rows, columns),
        aliases={5: 0},
    )(kept, rest_left, rest_right, left_env, right_env, total, second)
    moved_across, across, total = lax.optimization_barrier((moved_across, across, total))
    (total,) = call(
        late_kernel,
        [in_vmem] * 5,
        [total_shape],
        [],
        cost(charged_count, rows, rows, columns),
        aliases={4: 0},
    )(moved_across, upper, lower, across, total)
    (out,) = call(
        functools.partial(finish_kernel, right_count),
        [in_vmem] * 4,
        [pltpu.VMEM((rows, columns), bf16)],
        [pltpu.VMEM((rows, columns), bf16), sems(4)],
        None,
        out_specs=[in_hbm],
    )(total, first_received, relayed, second_received)
    return out


def solution(mesh):
    in_specs = (P("lsec", "rsec"), P(None, "lsec", None), P(None, "rsec", None))
    out_specs = P("lsec", "rsec")
    body = functools.partial(shards, mesh.shape["lsec"], mesh.shape["rsec"])
    return jax.shard_map(
        body, mesh=mesh, in_specs=in_specs, out_specs=out_specs, check_vma=False
    )
```

```python
import functools

import jax
import jax.numpy as jnp
from jax import lax
from jax.experimental import pallas as pl
from jax.experimental.pallas import tpu as pltpu
from jax.sharding import PartitionSpec as P


channel_shifts = (0, 1, -1, 0)
period = len(channel_shifts)
in_vmem = pl.BlockSpec(memory_space=pltpu.VMEM)
in_smem = pl.BlockSpec(memory_space=pltpu.SMEM)
in_hbm = pl.BlockSpec(memory_space=pl.ANY)


def contract(left_block, block, right_block):
    partial = jnp.dot(left_block, block, preferred_element_type=jnp.float32)
    return jnp.dot(
        partial.astype(jnp.bfloat16), right_block, preferred_element_type=jnp.float32
    )


def local_channel(step):
    return period * (step // 2) + (period - 1) * (step % 2)


def cost(steps, rows, inner, columns):
    macs = steps * (rows * inner * columns + rows * columns * columns)
    moved = 2 * steps * (rows * inner + columns * columns)
    return pl.CostEstimate(flops=2 * macs, bytes_accessed=moved, transcendentals=0)


class Fetch:
    def __init__(self, sems):
        self.sems, self.used = sems, 0

    def start(self, *pairs):
        copies = []
        for source, target in pairs:
            copies.append(pltpu.make_async_copy(source, target, self.sems.at[self.used]))
            self.used += 1
        for copy in copies:
            copy.start()
        return copies


def wait(copies):
    for copy in copies:
        copy.wait()


def half_blocks(left_ref, target_ref, charged, half):
    steps, part = target_ref.shape[:2]
    return [
        (left_ref.at[period * w + charged, pl.ds(half * part, part), :], target_ref.at[w])
        for w in range(steps)
    ]


def right_blocks(right_ref, target_ref, charged):
    return [
        (right_ref.at[period * w + charged], target_ref.at[w])
        for w in range(target_ref.shape[0])
    ]


def local_blocks(left_ref, right_ref, left_target, right_target, step, slot):
    channel = local_channel(step)
    return [
        (left_ref.at[channel], left_target.at[slot]),
        (right_ref.at[channel], right_target.at[slot]),
    ]


def spare_copies(left_ref, right_ref, left_target, right_target, step, half, sems):
    channel, part = local_channel(step), left_target.shape[0]
    rows = pl.ds(half * (left_ref.shape[1] - part), part)
    return [
        pltpu.make_async_copy(left_ref.at[channel, rows, :], left_target, sems.at[0]),
        pltpu.make_async_copy(right_ref.at[channel], right_target, sems.at[1]),
    ]


def local_kernel(right_count, spare_step, charged_ref, whole_ref, left_ref, right_ref, total_ref, psi_ref, next_left_ref,
                 lower_ref, next_right_ref, give_ref, lefts_ref, rights_ref, spare_left_ref,
                 spare_right_ref, sems, spare_sems):
    charged = charged_ref[0]
    fetch = Fetch(sems)
    steps = lefts_ref.shape[0]
    bring = lambda step: fetch.start(
        *local_blocks(left_ref, right_ref, lefts_ref, rights_ref, step, step)
    )
    coming = {0: fetch.start((whole_ref, psi_ref)) + bring(0)}
    last = []
    more = jnp.logical_not(takes_more(right_count))
    part = spare_left_ref.shape[0]
    spare = spare_copies(left_ref, right_ref, spare_left_ref, spare_right_ref, spare_step, 0,
                         spare_sems)
    for step in range(steps):
        wait(coming[step])
        for later in range(1, steps) if step == 0 else ():
            coming[later] = bring(later)
        if step == 1:
            last += fetch.start(*right_blocks(right_ref, next_right_ref, charged))
            last += fetch.start(*half_blocks(left_ref, next_left_ref, charged, 0))
            last += fetch.start(*half_blocks(left_ref, lower_ref, charged, 1))
            last += fetch.start(*right_blocks(right_ref, give_ref, period - 1 - charged))
        if step == 2:
            @pl.when(more)
            def _():
                for copy in spare:
                    copy.start()

        term = contract(lefts_ref[step], psi_ref[...], rights_ref[step])
        total_ref[...] = total_ref[...] + term if step else term

    @pl.when(more)
    def _():
        wait(spare)
        total_ref[:part, :] += contract(spare_left_ref[...], psi_ref[...], spare_right_ref[...])

    wait(last)


def early_term(psi_ref, lefts_ref, rights_ref, term_ref, total_ref):
    steps = lefts_ref.shape[0]
    for step in range(steps):
        term = contract(lefts_ref[step], psi_ref[...], rights_ref[step])
        total = total_ref[...] + term if step else term
        if step + 1 < steps:
            total_ref[...] = total
        else:
            term_ref[...] = total.astype(term_ref.dtype)


def at_edge(right_count):
    sector = lax.axis_index("rsec")
    return (sector == 0) | (sector == right_count - 1)


def early_or_local(early, local, step, kept_ref, psi_ref, lefts_ref, rights_ref, left_ref,
                   right_ref, term_ref, total_ref, work_ref, spare_left_ref, spare_right_ref,
                   sems):
    copies = [
        pltpu.make_async_copy(source, target, sems.at[index])
        for index, (source, target) in enumerate(local_blocks(
            left_ref, right_ref, spare_left_ref, spare_right_ref, step, 0))
    ]

    @pl.when(local)
    def _():
        for copy in copies:
            copy.start()

    @pl.when(early)
    def _():
        early_term(psi_ref, lefts_ref, rights_ref, term_ref, work_ref)

    @pl.when(local)
    def _():
        wait(copies)
        total_ref[...] += contract(spare_left_ref[0], kept_ref[...], spare_right_ref[0])


def takes_more(right_count):
    return at_edge(right_count) | (lax.rem(lax.axis_index("rsec"), 2) == 1)


def first_kernel(right_count, step, kept_ref, psi_ref, lefts_ref, rights_ref, left_ref,
                 right_ref, start_ref, term_ref, total_ref, work_ref, spare_left_ref,
                 spare_right_ref, sems):
    del start_ref
    early_or_local(jnp.logical_not(at_edge(right_count)), takes_more(right_count), step, kept_ref,
                   psi_ref, lefts_ref, rights_ref, left_ref, right_ref, term_ref, total_ref,
                   work_ref, spare_left_ref, spare_right_ref, sems)


def second_kernel(right_count, step, next_step, kept_ref, psi_ref, lefts_ref, rights_ref,
                  left_ref, right_ref, start_ref, after_ref, term_ref, total_ref, next_left_ref,
                  next_right_ref, work_ref, spare_left_ref, spare_right_ref, sems, next_sems):
    del start_ref, after_ref
    coming = Fetch(next_sems).start(*local_blocks(
        left_ref, right_ref, next_left_ref, next_right_ref, next_step, 0))
    edge = at_edge(right_count)
    early_or_local(jnp.logical_not(edge), edge, step, kept_ref, psi_ref, lefts_ref, rights_ref,
                   left_ref, right_ref, term_ref, total_ref, work_ref, spare_left_ref,
                   spare_right_ref, sems)
    wait(coming)


def rest_kernel(next_step, psi_ref, left0_ref, right0_ref, left_ref, right_ref, start_ref,
                after_ref, total_ref, next_left_ref, next_right_ref, sems):
    del start_ref, after_ref
    coming = Fetch(sems).start(*local_blocks(
        left_ref, right_ref, next_left_ref, next_right_ref, next_step, 0))
    total_ref[...] += contract(left0_ref[0], psi_ref[...], right0_ref[0])
    wait(coming)


def tail_kernel(right_count, step, psi_ref, left0_ref, right0_ref, left_ref, right_ref,
                start_ref, after_ref, total_ref, spare_left_ref, spare_right_ref, sems):
    del start_ref, after_ref
    more = jnp.logical_not(takes_more(right_count))
    part = spare_left_ref.shape[0]
    spare = spare_copies(left_ref, right_ref, spare_left_ref, spare_right_ref, step, 1, sems)

    @pl.when(more)
    def _():
        for copy in spare:
            copy.start()

    @pl.when(jnp.logical_not(at_edge(right_count)))
    def _():
        total_ref[...] += contract(left0_ref[0], psi_ref[...], right0_ref[0])

    @pl.when(more)
    def _():
        wait(spare)
        total_ref[total_ref.shape[0] - part:, :] += contract(
            spare_left_ref[...], psi_ref[...], spare_right_ref[...])


def late_kernel(moved_ref, upper_ref, lower_ref, across_ref, start_ref, total_ref):
    del start_ref
    part = upper_ref.shape[1]
    for index in range(across_ref.shape[0]):
        for rows, side_ref in ((slice(0, part), upper_ref), (slice(part, None), lower_ref)):
            total_ref[rows, :] += contract(side_ref[index], moved_ref[...], across_ref[index])


def finish_kernel(right_count, total_ref, first_ref, relay_ref, second_ref, out_ref, ready_ref,
                  sems):
    part = first_ref.shape[0]
    sector = lax.axis_index("rsec")
    middle = right_count // 2
    inner = (sector == middle - 1) | (sector == middle)
    relayed = inner | (sector == 0) | (sector == right_count - 1)
    puts, step = [], part // 2

    def put(offset, rows, received):
        target = pl.ds(offset + rows.start, step)
        total = total_ref[target, :] + received.astype(jnp.float32)
        ready_ref[target, :] = total.astype(ready_ref.dtype)
        puts.append(pltpu.make_async_copy(
            ready_ref.at[target, :], out_ref.at[target, :], sems.at[len(puts)]))
        puts[-1].start()

    pieces = [slice(0, step), slice(step, part)]
    for rows in pieces:
        put(part, rows, second_ref[rows, :])
    for rows in pieces:
        put(0, rows, jnp.where(relayed, relay_ref[rows, :], first_ref[rows, :]))
    wait(puts)


def routes(left_count, right_count):
    index = lambda i, j: i * right_count + j
    straight, crossed, partner, along, onward, relay = [], [], [], [], [], []
    middle, edge = right_count // 2, right_count - 1
    via = {middle - 1: edge, middle: 0}
    for i in range(left_count):
        for j in range(right_count):
            step = 1 if j % 2 == 0 else -1
            partner.append((index(i, j + step), index(i, j)))
            if not 0 <= i + step < left_count:
                continue
            straight.append((index(i + step, j), index(i, j)))
            crossed.append((index(i + step, j + step), index(i, j)))
            if 0 <= j - step < right_count:
                along.append((index(i, j), index(i, j - step)))
                onward.append((index(i, j), index(i, via.get(j, j - step))))
                if j in via:
                    relay.append((index(i, via[j]), index(i, j - step)))
    return straight, crossed, partner, along, onward, relay


def shards(left_count, right_count, psi, left_whole, right_whole):
    axes = ("lsec", "rsec")
    straight, crossed, partner, along, onward, relay = routes(left_count, right_count)
    rows, columns = psi.shape
    channels = left_whole.shape[0]
    charged_count = channels // period
    local_first = channels // 2 - 3
    part = rows // 2
    f32, bf16 = jnp.float32, jnp.bfloat16
    lefts = lambda count: pltpu.VMEM((count, rows, rows), bf16)
    halves = pltpu.VMEM((charged_count, part, rows), bf16)
    rights = lambda count: pltpu.VMEM((count, columns, columns), bf16)
    shape = lambda ref: jax.ShapeDtypeStruct(ref.shape, ref.dtype)
    sems = lambda count: pltpu.SemaphoreType.DMA((count,))

    def call(kernel, in_specs, outs, scratch, work, limit=20, aliases=None, out_specs=None):
        return pl.pallas_call(
            kernel,
            in_specs=in_specs,
            out_specs=out_specs or [in_vmem] * len(outs),
            out_shape=[shape(out) for out in outs],
            scratch_shapes=scratch,
            input_output_aliases=aliases or {},
            compiler_params=pltpu.CompilerParams(vmem_limit_bytes=limit << 20),
            cost_estimate=work,
        )

    charged = jnp.reshape(1 + lax.axis_index("rsec") % 2, (1,)).astype(jnp.int32)
    left_env = pltpu.with_memory_space_constraint(left_whole, pltpu.HBM)
    right_env = pltpu.with_memory_space_constraint(right_whole, pltpu.HBM)
    total_shape = pltpu.VMEM((rows, columns), f32)
    spare_rows = rows * 3 // 8
    spare = lambda count: [
        pltpu.VMEM((count, rows), bf16), pltpu.VMEM((columns, columns), bf16)]
    half_total = pltpu.VMEM((part, columns), f32)
    half_block = pltpu.VMEM((part, columns), bf16)

    moved = lax.ppermute(psi, axes, straight)

    total, kept, upper, lower, own, give = call(
        functools.partial(local_kernel, right_count, local_first + 2),
        [in_smem, in_hbm, in_hbm, in_hbm],
        [total_shape, pltpu.VMEM((rows, columns), bf16), halves, halves, rights(charged_count), rights(charged_count)],
        [lefts(local_first), rights(local_first), *spare(spare_rows),
         sems(2 * local_first + 1 + 4 * charged_count), sems(2)],
        cost(local_first, rows, rows, columns),
    )(charged, pltpu.with_memory_space_constraint(psi, pltpu.HBM), left_env, right_env)

    moved_across = lax.ppermute(kept, axes, crossed)
    moved, total = lax.optimization_barrier((moved, total))
    first, total = call(
        functools.partial(first_kernel, right_count, local_first + 2),
        [in_vmem] * 4 + [in_hbm, in_hbm, in_vmem],
        [half_block, total_shape],
        [half_total, lefts(1), rights(1), sems(2)],
        cost(charged_count, part, rows, columns),
        aliases={6: 1},
    )(kept, moved, upper, own, left_env, right_env, total)
    first_received = lax.ppermute(first, axes, onward)
    second, total, rest_left, rest_right = call(
        functools.partial(second_kernel, right_count, local_first + 1, local_first),
        [in_vmem] * 4 + [in_hbm, in_hbm, in_vmem, in_hbm],
        [half_block, total_shape, lefts(1), rights(1)],
        [half_total, lefts(1), rights(1), sems(2), sems(2)],
        cost(charged_count, part, rows, columns),
        aliases={6: 1},
    )(kept, moved, lower, own, left_env, right_env, total, first)
    second_received = lax.ppermute(second, axes, along)
    across = lax.ppermute(give, axes, partner)
    total, rest_left, rest_right = call(
        functools.partial(rest_kernel, local_first + 1),
        [in_vmem, in_vmem, in_vmem, in_hbm, in_hbm, in_vmem, in_hbm],
        [total_shape, lefts(1), rights(1)],
        [sems(2)],
        cost(1, rows, rows, columns),
        aliases={5: 0},
    )(kept, rest_left, rest_right, left_env, right_env, total, second)
    first_received, total = lax.optimization_barrier((first_received, total))
    relayed = lax.ppermute(first_received, axes, relay)

    (total,) = call(
        functools.partial(tail_kernel, right_count, local_first + 2),
        [in_vmem] * 3 + [in_hbm, in_hbm, in_vmem, in_hbm],
        [total_shape],
        [*spare(rows - spare_rows), sems(2)],
        cost(2, rows, rows, columns),
        aliases={5: 0},
    )(kept, rest_left, rest_right, left_env, right_env, total, second)
    moved_across, across, total = lax.optimization_barrier((moved_across, across, total))
    (total,) = call(
        late_kernel,
        [in_vmem] * 5,
        [total_shape],
        [],
        cost(charged_count, rows, rows, columns),
        aliases={4: 0},
    )(moved_across, upper, lower, across, total)
    (out,) = call(
        functools.partial(finish_kernel, right_count),
        [in_vmem] * 4,
        [pltpu.VMEM((rows, columns), bf16)],
        [pltpu.VMEM((rows, columns), bf16), sems(4)],
        None,
        out_specs=[in_hbm],
    )(total, first_received, relayed, second_received)
    return out


def solution(mesh):
    in_specs = (P("lsec", "rsec"), P(None, "lsec", None), P(None, "rsec", None))
    out_specs = P("lsec", "rsec")
    body = functools.partial(shards, mesh.shape["lsec"], mesh.shape["rsec"])
    return jax.shard_map(
        body, mesh=mesh, in_specs=in_specs, out_specs=out_specs, check_vma=False
    )
```
